512 devices in a mesh: req: 16 (over z, core), seq: 32 (over y, x).
Axes of the slice: x: 4, y: 8, z: 8, core: 2. Of those that a mesh axis runs over, the one named last changes fastest.
Arguments:
- queries: bfloat16 [16, 128, 4096], P('req', 'seq'), may hold values from -160 to 160
- kv_cache: bfloat16 [16, 16384, 2, 256], P('req', 'seq'), may hold values from -6 to 6
- tree_kv: bfloat16 [16, 128, 2, 256], P('req', 'seq'), may hold values from -14 to 14
- context_lengths: int32 [16], P('req'), may hold values from 2048 to 16384, as said below
- tree_parents: int32 [16, 128], P('req'), may hold values from -1 to 126, as said below
- resid: bfloat16 [16, 128, 4096], P('req', 'seq'), may hold values from -6 to 6
- out_weight: bfloat16 [4096, 4096], P('seq'), may hold values from -0.5 to 0.5
- norm_gain: bfloat16 [4096], replicated, may hold values from 0.099609375 to 1.8984375
- expert_ids: int32 [16, 128, 8], P('req'), may hold values from 0 to 63, all different within a row; in each aligned block of 128 rows (0 to 127, 128 to 255, ..., all dimensions but the last counted through in order) at most 32 rows name the same one
- gate_weights: bfloat16 [16, 128, 8], P('req'), may hold values from 0.049804688 to 0.5
- w_gate: bfloat16 [512, 4096, 128], P(('req', 'seq')), may hold values from -0.09375 to 0.09375
- w_up: bfloat16 [512, 4096, 128], P(('req', 'seq')), may hold values from -0.09375 to 0.09375
- w_down: bfloat16 [512, 128, 4096], P(('req', 'seq')), may hold values from -0.375 to 0.375
Outputs:
- attended: bfloat16 [16, 128, 4096], P('req', 'seq')
- expert_sum: bfloat16 [16, 128, 4096], P('req', 'seq')
The draws below stay inside these ranges and needn't reach their ends.
Inputs may be any that keep to these rules, and one draw needn't show every extreme that they name: `expert_ids`: each row names 8 different experts; among the rows of one request no expert is named by more than 32 rows. `tree_parents`: each request holds 4 trees of 32 nodes in a row; a tree's first node has parent -1, every other node's parent is an earlier node of the same tree; the request's last node has parent 128 - 2. `context_lengths`: at least one request uses all 16384 positions.
All inputs are finite; a program needn't handle non-finite values.
Results may differ from the reference program's by a relative error of at most 0.01615.
Values may be sent and summed in bfloat16 or wider, within the bound.
A program may use at most 64 MiB of HBM per device.

```python
import math
import jax
import jax.numpy as jnp
import numpy as np
from jax import lax

D = 4096
DH = 128
HQ = 32
KVH = 2
EXPERTS = 64
FF_WIN = 1024
HID_DEV = 128
TOPK = 8
TREE = 32
CAP = 32
C_DEV = 512
ROWS = 128
SPLIT = 8
PANELS = 512
CTX = 16384
REQUESTS = 16
N_SEQ = 32


def cache_base(key):
    base = jax.random.normal(jax.random.fold_in(key, 11), (REQUESTS, CTX, 2, KVH * DH), jnp.float32)
    return jnp.clip(base, -6.0, 6.0)


def draw_kv_cache(key, part):
    base = cache_base(key)
    return base.astype(jnp.bfloat16)


def draw_queries(key, part):
    base = jax.random.normal(jax.random.fold_in(key, 12), (REQUESTS, ROWS, HQ * DH), jnp.float32)
    base = jnp.clip(base, -6.0, 6.0)
    return base.astype(jnp.bfloat16)


def draw_context_lengths(key, part):
    lengths = jax.random.randint(jax.random.fold_in(key, 21), (REQUESTS,), CTX // 8, CTX + 1)
    which = jax.random.randint(jax.random.fold_in(key, 22), (), 0, REQUESTS)
    return jnp.where(jnp.arange(REQUESTS) == which, CTX, lengths).astype(jnp.int32)


def draw_tree_parents(key, part):
    node = jnp.arange(ROWS, dtype=jnp.int32)
    local = node % TREE
    first = node - local
    raw = jax.random.randint(jax.random.fold_in(key, 31), (REQUESTS, ROWS), 0, 1048576)
    chosen = raw % jnp.maximum(local, 1)[None, :]
    parents = jnp.where(local[None, :] == 0, -1, first[None, :] + chosen)
    parents = jnp.where(node[None, :] == ROWS - 1, ROWS - 2, parents)
    return parents.astype(jnp.int32)


def steps_of(own_key, dims, split, low, largest):
    gain, own = 1.0, jax.random.fold_in(own_key, 6)
    for axis_at, parts in split:
        draws = jnp.exp(jax.random.uniform(jax.random.fold_in(own, axis_at), (parts,), jnp.float32, low / len(split), largest / len(split)))
        gain = gain * jnp.repeat(draws, dims[axis_at] // parts).reshape([-1 if axis == axis_at else 1 for axis in range(len(dims))])
    return gain


def shared_out(key, own, number, rows, count, top, bound, lean):
    sequence = jax.random.permutation(key, count)
    heavy_load, usual = load_shares(count, rows * top, bound, lean, True), load_shares(count, rows * top, bound, lean, False)
    places = jnp.arange(count)

    def named(sizes, rotation):
        used = int((sizes > 0).sum())
        fixed = max(1, used // 4)
        passed = fixed + (places - fixed + rotation * (used - fixed)) % max(1, count - fixed)
        return jnp.zeros((count,), jnp.int32).at[sequence[jnp.where(places < fixed, places, passed)]].set(jnp.asarray(sizes, jnp.int32))

    sizes = jnp.where(number % 4 == 0, named(heavy_load, number // 4), named(usual, number - number // 4 - 1))
    mixed = jax.random.permutation(jax.random.fold_in(own, 3), count)
    donor, sink = mixed[0:count // 2 * 2:2], mixed[1:count // 2 * 2:2]
    slack = jnp.minimum(sizes[donor] - 1, bound - sizes[sink]) // 2
    slack = jnp.where((donor == sequence[0]) | (sink == sequence[0]) | (sizes[sink] == 0), 0, jnp.maximum(slack, 0))
    passed = jax.random.randint(jax.random.fold_in(own, 4), (count // 2,), 0, 1 << 20) % (slack + 1)
    sizes = sizes.at[donor].add(-passed).at[sink].add(passed)
    items = jnp.searchsorted(jnp.cumsum(sizes), jnp.arange(rows * top), side="right").astype(jnp.int32)
    listing = items.reshape(top, rows).T
    listing = listing[jax.random.permutation(jax.random.fold_in(own, 1), rows)]
    rotation = jax.random.randint(jax.random.fold_in(own, 2), (rows, 1), 0, top)
    return jnp.take_along_axis(listing, (jnp.arange(top)[None, :] + rotation) % top, axis=1)


def load_shares(number_of, total, limit, lean, full):
    loads = [(1 << 20) // math.isqrt(rank ** lean) + 1 for rank in range(1, number_of + 1)]
    largest = limit if full else min(limit, max(-(-total // number_of), total * loads[0] // sum(loads)))
    least = 1 if total - largest >= number_of - 1 else 0
    counts, rest = [largest] + [least] * (number_of - 1), total - largest - least * (number_of - 1)
    while rest > 0:
        movable = [i for i in range(1, number_of) if counts[i] < largest] or [i for i in range(1, number_of) if counts[i] < limit]
        mass, left = sum([loads[i] for i in movable]), rest
        for i in movable:
            addition = min(limit - counts[i], max(1, left * loads[i] // mass), rest)
            counts[i] = counts[i] + addition
            rest = rest - addition
    return np.array(counts)


def scatter_about(own_key, dims, spread, bound, cuts=(), held_as=jnp.bfloat16):
    loudness = steps_of(own_key, dims, cuts, -0.22, 0.18) if cuts else 1.0
    values = jax.random.normal(own_key, dims, jnp.float32) * spread * loudness
    return jnp.minimum(jnp.maximum(values, -bound), bound).astype(held_as)


def setup_inputs(seed: int = 0) -> dict:
    seeds = jax.random.split(jax.random.key(seed), 14)
    queries = draw_queries(jax.random.fold_in(seeds[13], 71), 0)
    kv_cache = draw_kv_cache(jax.random.fold_in(seeds[13], 71), 0)
    tree_kv = scatter_about(seeds[2], (REQUESTS, ROWS, 2, KVH * DH), 3.5, 14.0, ((0, 16), (1, 32)))
    context_lengths = draw_context_lengths(jax.random.fold_in(seeds[13], 71), 0)
    tree_parents = draw_tree_parents(jax.random.fold_in(seeds[13], 71), 0)
    resid = scatter_about(seeds[5], (REQUESTS, ROWS, D), 1.0, 6.0, ((0, 16), (1, 32)))
    out_weight = scatter_about(seeds[6], (HQ * DH, D), 0.08, 0.5, ((0, 32),))
    norm_gain = jnp.clip(1.0 + 0.18 * jax.random.normal(seeds[7], (D,), jnp.float32), 0.099609375, 1.8984375).astype(jnp.bfloat16)
    expert_ids_keys = jax.random.split(jax.random.fold_in(seeds[8], 1), REQUESTS * ROWS // ROWS)
    expert_ids_turns = jax.random.permutation(jax.random.fold_in(seeds[8], 3), REQUESTS * ROWS // ROWS)
    expert_ids = jax.vmap(lambda own, number: shared_out(jax.random.fold_in(seeds[8], 2), own, number, ROWS, EXPERTS, TOPK, CAP, 1))(expert_ids_keys, expert_ids_turns).reshape((REQUESTS, ROWS, TOPK))
    gate_weights = jnp.clip(jnp.exp(math.log(0.5) - 2.306499 * jax.random.uniform(seeds[9], (REQUESTS, ROWS, TOPK), jnp.float32) ** steps_of(seeds[9], (REQUESTS, ROWS, TOPK), ((0, 16),), -0.2, 0.2)), 0.049804688, 0.5).astype(jnp.bfloat16)
    w_gate = scatter_about(seeds[10], (PANELS, D, HID_DEV), D ** -0.5, 0.09375, ((0, 512),))
    w_up = scatter_about(seeds[11], (PANELS, D, HID_DEV), D ** -0.5, 0.09375, ((0, 512),))
    w_down = scatter_about(seeds[12], (PANELS, HID_DEV, D), (FF_WIN // 4) ** -0.5, 0.375, ((0, 512),))
    return {"queries": queries, "kv_cache": kv_cache, "tree_kv": tree_kv, "context_lengths": context_lengths, "tree_parents": tree_parents, "resid": resid, "out_weight": out_weight, "norm_gain": norm_gain, "expert_ids": expert_ids, "gate_weights": gate_weights, "w_gate": w_gate, "w_up": w_up, "w_down": w_down}


NEG = -1e+30
EPS = 1e-06

def ancestry(parents):
    count = parents.shape[0]
    node = jnp.arange(count, dtype=jnp.int32)
    linked = (parents[:, None] == node[None, :]) | (node[:, None] == node[None, :])
    reach = linked.astype(jnp.float32)
    hops = 1
    while hops < count:
        reach = jnp.minimum(jnp.dot(reach, reach, preferred_element_type=jnp.float32), 1.0)
        hops = hops * 2
    return reach > 0.5

def rounded(value):
    return lax.optimization_barrier(value.astype(jnp.bfloat16)).astype(jnp.float32)

def attend(query, cache, tree, length, parents):
    group = HQ // KVH
    scale = DH ** (-0.5)
    heads = query.astype(jnp.float32).reshape(ROWS, KVH, group, DH)

    def shard(carry, index):
        block = lax.dynamic_slice_in_dim(cache, (index * C_DEV).astype(jnp.int32), C_DEV, 0).astype(jnp.float32)
        keys = block[:, 0].reshape(C_DEV, KVH, DH)
        values = block[:, 1].reshape(C_DEV, KVH, DH)
        scores = jnp.einsum('rkgd,tkd->rkgt', heads, keys) * scale
        valid = index * C_DEV + jnp.arange(C_DEV, dtype=jnp.int32) < length
        top = lax.optimization_barrier(jnp.max(jnp.where(valid, scores, NEG), axis=-1))
        weights = jnp.where(valid, jnp.exp(scores - top[..., None]), 0.0)
        total = lax.optimization_barrier(jnp.sum(weights, axis=-1))
        out = jnp.einsum('rkgt,tkd->rkgd', rounded(weights), values)
        return (carry, (top, total, out))
    _, (tops, totals, outs) = lax.scan(shard, jnp.int32(0), jnp.arange(N_SEQ, dtype=jnp.int32))
    tree_f = tree.astype(jnp.float32)
    tree_keys = tree_f[:, 0].reshape(ROWS, KVH, DH)
    tree_vals = tree_f[:, 1].reshape(ROWS, KVH, DH)
    tree_scores = jnp.einsum('rkgd,nkd->rkgn', heads, tree_keys) * scale
    linked = ancestry(parents)[:, None, None, :]
    tree_top = lax.optimization_barrier(jnp.max(jnp.where(linked, tree_scores, NEG), axis=-1))
    tree_weights = jnp.where(linked, jnp.exp(tree_scores - tree_top[..., None]), 0.0)
    tree_total = lax.optimization_barrier(jnp.sum(tree_weights, axis=-1))
    tree_out = jnp.einsum('rkgn,nkd->rkgd', rounded(tree_weights), tree_vals)
    peak = jnp.maximum(lax.optimization_barrier(jnp.max(tops, axis=0)), tree_top)
    factor = jnp.exp(tops - peak[None])
    tree_factor = jnp.exp(tree_top - peak)
    numer = lax.optimization_barrier(jnp.sum(factor[..., None] * outs, axis=0)) + tree_factor[..., None] * tree_out
    denom = lax.optimization_barrier(jnp.sum(factor * totals, axis=0)) + tree_factor * tree_total
    return (numer / denom[..., None]).astype(jnp.bfloat16).reshape(ROWS, HQ * DH)

def route(ids, gates):
    table = jnp.arange(EXPERTS, dtype=jnp.int32)
    hits = ids[:, :, None] == table[None, None, :]
    choose = lax.optimization_barrier(jnp.sum(hits.astype(jnp.int32), axis=1))
    weight = lax.optimization_barrier(jnp.sum(jnp.where(hits, gates.astype(jnp.float32)[:, :, None], 0.0), axis=1))
    slot = jnp.cumsum(choose, axis=0) - choose
    return (choose, weight, slot)

def reference(queries, kv_cache, tree_kv, context_lengths, tree_parents, resid, out_weight, norm_gain, expert_ids, gate_weights, w_gate, w_up, w_down):

    def one_request(packed):
        query, cache, tree, length, parents, base = packed
        attention = attend(query, cache, tree, length, parents)
        attended = jnp.dot(attention, out_weight, preferred_element_type=jnp.float32).astype(jnp.bfloat16)
        midf = rounded(base.astype(jnp.float32) + attended.astype(jnp.float32))
        factor = lax.rsqrt(lax.optimization_barrier(jnp.mean(midf * midf, axis=-1, keepdims=True)) + EPS)
        normed = (midf * factor * norm_gain.astype(jnp.float32)).astype(jnp.bfloat16)
        return (attended, normed)
    attended, normed = lax.map(one_request, (queries, kv_cache, tree_kv, context_lengths, tree_parents, resid))
    choose, weight, slot = jax.vmap(route)(expert_ids, gate_weights)
    normed_f = normed.astype(jnp.float32)
    seats = jnp.arange(CAP, dtype=jnp.int32)

    def expert_step(total, expert):
        picked = jnp.arange(EXPERTS, dtype=jnp.int32) == expert
        col_choose = lax.optimization_barrier(jnp.sum(jnp.where(picked, choose, 0), axis=-1))
        col_slot = lax.optimization_barrier(jnp.sum(jnp.where(picked, slot, 0), axis=-1))
        col_weight = lax.optimization_barrier(jnp.sum(jnp.where(picked, weight, 0.0), axis=-1))
        select = ((col_choose[:, None, :] > 0) & (col_slot[:, None, :] == seats[None, :, None])).astype(jnp.float32)
        rows = jnp.einsum('bci,bid->bcd', select, normed_f)
        rates = jnp.einsum('bci,bi->bc', select, col_weight)
        first = (expert * SPLIT).astype(jnp.int32)
        wg = lax.dynamic_slice_in_dim(w_gate, first, SPLIT, 0).astype(jnp.float32)
        wu = lax.dynamic_slice_in_dim(w_up, first, SPLIT, 0).astype(jnp.float32)
        wd = lax.dynamic_slice_in_dim(w_down, first, SPLIT, 0).astype(jnp.float32)
        gate = jnp.einsum('bcd,kdh->bckh', rows, wg)
        up = jnp.einsum('bcd,kdh->bckh', rows, wu)
        hidden = rounded(jax.nn.silu(gate) * up * rates[:, :, None, None])
        part = rounded(jnp.einsum('bckh,khd->bckd', hidden, wd))
        return (total + jnp.einsum('bci,bckd->bid', select, part), None)
    start = jnp.zeros((REQUESTS, ROWS, D), jnp.float32)
    total, _ = lax.scan(expert_step, start, jnp.arange(EXPERTS, dtype=jnp.int32))
    return (attended, total.astype(jnp.bfloat16))
```

```python
import jax
import jax.numpy as jnp
from jax import lax
from jax.experimental import pallas as pl
from jax.experimental.pallas import tpu as pltpu
from jax.sharding import PartitionSpec as P

BF = jnp.bfloat16
F32 = jnp.float32
MESH = pl.DeviceIdType.MESH
NX, NY = 4, 8
NR, NS = 16, 32
SPAN = 528
KEYS = 2 * SPAN
MASKED = -1e30
FLOOR = -1e29
EPS = 1e-06


def rem(a, b):
    return lax.rem(a, jnp.int32(b))


def div(a, b):
    return lax.div(a, jnp.int32(b))


def place():
    r = lax.axis_index("req")
    s = lax.axis_index("seq")
    return r, s, rem(s, NX), div(s, NX)


def remote(src, dst, send, recv, r, s):
    return pltpu.make_async_remote_copy(
        src_ref=src, dst_ref=dst, send_sem=send, recv_sem=recv, device_id=(r, s), device_id_type=MESH
    )


def loop(n, first=0):
    def run(fn):
        def step(i, c):
            fn(i)
            return c

        lax.fori_loop(first, n, step, 0)

    return run


def dot(a, b):
    return jnp.dot(a, b, preferred_element_type=F32)


def gather_kernel(q_in, kv_in, res_in, link, q_out, kv_out, res_out, reach_out,
                  qy, reach, ys, yr, xs, xr, ks, rs, rr, ls):
    r, s, x, y = place()
    h = rem(x, 2)
    mate = s + 1 - 2 * h
    barrier = pltpu.get_barrier_semaphore()

    @loop(NS, 1)
    def _(d):
        pl.semaphore_signal(barrier, inc=1, device_id=(r, rem(s + d, NS)), device_id_type=MESH)

    pl.semaphore_wait(barrier, NS - 1)

    def y_copy(d):
        return remote(q_in, qy.at[y], ys.at[d], yr.at[d], r, rem(y + d, NY) * NX + x)

    def kv_copy():
        return remote(kv_in.at[1 - h], kv_out.at[h], ks.at[0], ks.at[1], r, mate)

    def res_copy(d):
        to = rem(s + d, NS)
        return remote(res_in.at[to], res_out.at[s], rs.at[d], rr.at[d], r, to)

    def x_copy(d, e):
        row = rem(y + NY - d, NY)
        to = rem(x + e, NX)
        return remote(qy.at[row, rem(to, 2)], q_out.at[row * NX + x], xs.at[d, e], xr.at[d, e], r, y * NX + to)

    @loop(NY, 1)
    def _(d):
        y_copy(d).start()

    kv_copy().start()
    own_q = pltpu.make_async_copy(q_in, qy.at[y], ls.at[0])
    own_q.start()
    own_kv = pltpu.make_async_copy(kv_in.at[h], kv_out.at[h], ls.at[1])
    own_kv.start()
    own_res = pltpu.make_async_copy(res_in.at[s], res_out.at[s], ls.at[2])
    own_res.start()
    own_q.wait()

    def spread(d):
        for e in range(1, NX):
            x_copy(d, e).start()
        row = rem(y + NY - d, NY)
        pltpu.make_async_copy(qy.at[row, h], q_out.at[row * NX + x], xs.at[d, 0]).start()

    spread(0)

    @loop(NS, 1)
    def _(d):
        res_copy(d).start()

    @loop(NY, 1)
    def _(d):
        y_copy(d).wait_recv()
        spread(d)

    reach[...] = link[...]

    @loop(5)
    def _(i):
        reach[...] = jnp.minimum(dot(reach[...], reach[...]), 1.0).astype(BF)

    reach_out[...] = reach[...]
    own_kv.wait()
    own_res.wait()
    kv_copy().wait()

    @loop(NY, 1)
    def _(d):
        y_copy(d).wait_send()

    @loop(NS, 1)
    def _(d):
        res_copy(d).wait()

    @loop(NY)
    def _(d):
        for e in range(1, NX):
            x_copy(d, e).wait()
        row = rem(y + NY - d, NY)
        pltpu.make_async_copy(qy.at[row, h], q_out.at[row * NX + x], xs.at[d, 0]).wait()


def main_kernel(
    q, k, vt, bias, res, w_out, gain, sel, back, w_gate, w_up, w_down,
    a_out, e_out,
    out_src, st_src, got, got_st, p_src, p_got, y_src, y_got, a_src, sq_src, sq, mid_src, mid_q,
    d_src, rows, wgu, wd, gu_src, gu, hid_src, hid, pair_src, pair, ret_src, ret, f_src, fin,
    hs, hr, ts, tr, ps, pr, ys, yr, as_, ar, qs, qr, ms, mr, zs, zr, fs, fr,
    gs, gr, us, ur, ds_, dr, gus, gur, hds, hdr, pas, par, bs, br, es, er, ls,
):
    r, s, x, y = place()
    h = rem(x, 2)
    b = rem(y, 2)
    top = div(y, 4)
    mate = s + NX - 2 * NX * b
    number = y * 2 + div(x, 2)
    barrier = pltpu.get_barrier_semaphore()

    @loop(NS, 1)
    def _(d):
        pl.semaphore_signal(barrier, inc=1, device_id=(r, rem(s + d, NS)), device_id_type=MESH)

    @loop(NR, 1)
    def _(d):
        pl.semaphore_signal(barrier, inc=1, device_id=(rem(r + d, NR), s), device_id_type=MESH)

    pl.semaphore_wait(barrier, NS + NR - 2)

    def x_at(e):
        return rem(x + e, NX)

    def gate_copy(e):
        to = x_at(e)
        return remote(w_gate.at[to], wgu.at[x, :, pl.ds(0, 128)], gs.at[e], gr.at[e], r, y * NX + to)

    def up_copy(e):
        to = x_at(e)
        return remote(w_up.at[to], wgu.at[x, :, pl.ds(128, 128)], us.at[e], ur.at[e], r, y * NX + to)

    def down_copy(e):
        to = x_at(e)
        return remote(
            w_down.at[:, pl.ds(pl.multiple_of(to * 1024, 1024), 1024)], wd.at[x], ds_.at[e], dr.at[e], r, y * NX + to
        )

    own_g = pltpu.make_async_copy(w_gate.at[x], wgu.at[x, :, pl.ds(0, 128)], ls.at[0])
    own_u = pltpu.make_async_copy(w_up.at[x], wgu.at[x, :, pl.ds(128, 128)], ls.at[1])
    own_d = pltpu.make_async_copy(w_down.at[:, pl.ds(pl.multiple_of(x * 1024, 1024), 1024)], wd.at[x], ls.at[2])
    own_g.start()
    own_u.start()
    own_d.start()

    def out_copy(i):
        return remote(out_src.at[i], got.at[number], hs.at[i], hr.at[number], r, 16 * h + i)

    def st_copy(i):
        return remote(st_src.at[i], got_st.at[number], ts.at[i], tr.at[number], r, 16 * h + i)

    def local_out(i):
        return (
            pltpu.make_async_copy(out_src.at[i], got.at[number], hs.at[i]),
            pltpu.make_async_copy(st_src.at[i], got_st.at[number], ts.at[i]),
        )

    def head_at(n):
        return rem(n + number, 16)

    def send_head(i):
        @pl.when(16 * h + i != s)
        def _():
            out_copy(i).start()
            st_copy(i).start()

        @pl.when(16 * h + i == s)
        def _():
            one, two = local_out(i)
            one.start()
            two.start()

    @loop(16)
    def _(n):
        i = head_at(n)
        heads = q[:, pl.ds(pl.multiple_of(i * 128, 128), 128)]
        score = lax.dot_general(k[...], heads, (((1,), (1,)), ((), ())), preferred_element_type=F32)
        score = score * (128 ** (-0.5)) + bias[...]
        peak = jnp.maximum(jnp.max(score, axis=0, keepdims=True), FLOOR)
        prob = jnp.exp(score - peak)
        total = jnp.sum(prob, axis=0, keepdims=True)
        out_src[i] = dot(vt[...], prob.astype(BF)).astype(BF)
        st_src[i] = jnp.concatenate([jnp.broadcast_to(peak, (8, 128)), jnp.broadcast_to(total, (8, 128))], axis=0)

        @pl.when(n >= 1)
        def _():
            send_head(head_at(n + 15))

    send_head(head_at(jnp.int32(15)))

    for e in range(1, NX):
        gate_copy(jnp.int32(e)).start()

    def wait_source(n):
        who = div(n, 2) * NX + 2 * rem(n, 2) + top

        @pl.when(who != s)
        def _():
            remote(out_src.at[0], got.at[n], hs.at[0], hr.at[n], r, who).wait_recv()
            remote(st_src.at[0], got_st.at[n], ts.at[0], tr.at[n], r, who).wait_recv()

    @loop(16)
    def _(n):
        wait_source(n)

    @loop(16)
    def _(n):
        i = head_at(n)

        @pl.when(16 * h + i != s)
        def _():
            out_copy(i).wait_send()
            st_copy(i).wait_send()

        @pl.when(16 * h + i == s)
        def _():
            one, two = local_out(i)
            one.wait()
            two.wait()

    peaks = got_st[:, 0:1, :]
    totals = got_st[:, 8:9, :]
    peak = jnp.max(peaks, axis=0)
    factor = jnp.exp(peaks - peak[None])
    denom = jnp.sum(factor * totals, axis=0)
    numer = jnp.zeros((128, 128), F32)
    for n in range(16):
        numer = numer + factor[n] * got[n].astype(F32)
    att = jnp.transpose(numer / denom).astype(BF)

    def p_copy(e):
        return remote(p_src.at[e], p_got.at[e], ps.at[e], pr.at[e], r, y * NX + x_at(e))

    for e in (1, 2, 3, 0):
        cols = pl.multiple_of(x_at(jnp.int32(e)) * 1024, 1024)
        part = dot(att, w_out[:, pl.ds(cols, 1024)]).astype(BF)
        p_src[e] = part
        if e:
            p_copy(e).start()
    for e in range(1, NX):
        up_copy(jnp.int32(e)).start()
    for e in range(1, NX):
        down_copy(jnp.int32(e)).start()
    for e in range(1, NX):
        p_copy(e).wait_recv()

    def y_copy(d):
        to = rem(y + d, NY)
        return remote(y_src.at[to], y_got.at[d], ys.at[d], yr.at[d], r, to * NX + x)

    for t in range(NY):
        c = slice(128 * t, 128 * t + 128)
        acc = p_src[0, :, c].astype(F32)
        for e in range(1, NX):
            acc = acc + p_got[e, :, c].astype(F32)
        y_src[t] = acc.astype(BF)

    @loop(NY, 1)
    def _(d):
        y_copy(d).start()

    acc = y_src[y].astype(F32)
    for d in range(1, NY):
        y_copy(jnp.int32(d)).wait_recv()
        acc = acc + y_got[d].astype(F32)
    attended = acc.astype(BF)
    mid = (res[...].astype(F32) + attended.astype(F32)).astype(BF)
    midf = mid.astype(F32)
    mid_src[...] = mid
    col = jnp.sum(midf * midf, axis=1, keepdims=True)
    sq_src[...] = jnp.transpose(jnp.broadcast_to(col, (128, 128)))[0:8, :]
    sq[s] = sq_src[...]
    wide = attended.astype(F32)
    for t in range(NS):
        a_src[t] = wide[4 * t : 4 * t + 4, :].astype(BF)

    def mid_copy(j):
        to = (2 * j + top) * NX + x
        return remote(mid_src, mid_q.at[rem(y, 4)], ms.at[j], mr.at[rem(y, 4)], r, to)

    def sq_copy(d):
        return remote(sq_src, sq.at[s], qs.at[d], qr.at[d], r, rem(s + d, NS))

    def a_copy(d):
        to = rem(s + d, NS)
        return remote(a_src.at[to], a_out.at[s], as_.at[d], ar.at[d], r, to)

    mine = pltpu.make_async_copy(mid_src, mid_q.at[rem(y, 4)], ls.at[3])

    @loop(NS, 1)
    def _(d):
        sq_copy(d).start()

    @loop(4)
    def _(j):
        @pl.when(2 * j + top != y)
        def _():
            mid_copy(j).start()

        @pl.when(2 * j + top == y)
        def _():
            mine.start()

    a_out[s] = a_src[s]

    @loop(NS, 1)
    def _(d):
        a_copy(d).start()

    @loop(4)
    def _(t):
        @pl.when(4 * b + t != y)
        def _():
            remote(mid_src, mid_q.at[t], ms.at[0], mr.at[t], r, (4 * b + t) * NX + x).wait_recv()

        @pl.when(4 * b + t == y)
        def _():
            mine.wait()

    @loop(NS, 1)
    def _(d):
        sq_copy(d).wait_recv()

    square = jnp.sum(sq[:, 0:1, :], axis=0)
    scale = lax.rsqrt(square * (1.0 / 4096.0) + EPS)
    scale = jnp.transpose(jnp.broadcast_to(scale, (128, 128)))
    for t in range(4):
        normed = (mid_q[t].astype(F32) * scale * gain[t]).astype(BF)
        d_src[:, :, 128 * t : 128 * t + 128] = dot(sel[...], normed).astype(BF).reshape(16, 32, 128)

    def z_copy(d):
        to = rem(r + d, NR)
        return remote(d_src.at[to], rows.at[b, r], zs.at[d], zr.at[d], to, s)

    def pass_copy(d):
        who = rem(r + NR - d, NR)
        return remote(rows.at[b, who], rows.at[b, who], fs.at[d], fr.at[d], r, mate)

    own_rows = pltpu.make_async_copy(d_src.at[r], rows.at[b, r], ls.at[4])
    own_rows.start()

    @loop(NR, 1)
    def _(d):
        z_copy(d).start()

    own_rows.wait()
    pass_copy(jnp.int32(0)).start()

    @loop(NR, 1)
    def _(d):
        z_copy(d).wait_recv()
        pass_copy(d).start()

    own_g.wait()
    own_u.wait()
    own_d.wait()
    for e in range(1, NX):
        gate_copy(jnp.int32(e)).wait()
        up_copy(jnp.int32(e)).wait()

    @loop(NR)
    def _(d):
        who = rem(r + NR - d, NR)
        remote(rows.at[1 - b, who], rows.at[1 - b, who], fs.at[d], fr.at[d], r, mate).wait_recv()

    def gu_copy(e):
        return remote(gu_src.at[e], gu.at[e], gus.at[e], gur.at[e], r, y * NX + x_at(e))

    for e in (1, 2, 3, 0):
        to = x_at(jnp.int32(e))

        @loop(4)
        def _(m):
            left = rows[0, pl.ds(4 * m, 4)].reshape(128, 512)
            right = rows[1, pl.ds(4 * m, 4)].reshape(128, 512)
            part = dot(left, wgu[to, 0:512, :]) + dot(right, wgu[to, 512:1024, :])
            gu_src[e, pl.ds(pl.multiple_of(128 * m, 128), 128), :] = part.astype(BF)

        if e:
            gu_copy(e).start()
    for e in range(1, NX):
        gu_copy(e).wait_recv()

    @loop(4)
    def _(m):
        part = pl.ds(pl.multiple_of(128 * m, 128), 128)
        acc = gu_src[0, part, :].astype(F32)
        for e in range(1, NX):
            acc = acc + gu[e, part, :].astype(F32)
        gate = acc[:, 0:128]
        hid_src[part, :] = (gate / (1.0 + jnp.exp(-gate)) * acc[:, 128:256]).astype(BF)

    def hid_copy(e):
        return remote(hid_src, hid.at[x], hds.at[e], hdr.at[e], r, y * NX + x_at(e))

    own_hid = pltpu.make_async_copy(hid_src, hid.at[x], ls.at[5])
    own_hid.start()
    for e in range(1, NX):
        hid_copy(e).start()
    for e in range(1, NX):
        down_copy(jnp.int32(e)).wait()
    own_hid.wait()
    for e in range(1, NX):
        hid_copy(e).wait_recv()

    def down(m, half):
        part = pl.ds(pl.multiple_of(128 * m, 128), 128)
        cols = pl.ds(pl.multiple_of(half * 512, 512), 512)
        acc = dot(hid[0, part, :], wd[0, :, cols])
        for t in range(1, NX):
            acc = acc + dot(hid[t, part, :], wd[t, :, cols])
        return acc

    def pair_copy(m):
        part = pl.ds(pl.multiple_of(128 * m, 128), 128)
        return remote(pair_src.at[part], pair.at[part], pas.at[m], par.at[m], r, mate)

    @loop(4)
    def _(m):
        part = pl.ds(pl.multiple_of(128 * m, 128), 128)
        pair_src[part, :] = down(m, 1 - b).astype(BF)
        pair_copy(m).start()

    def b_copy(to):
        return remote(ret_src.at[to], ret.at[r], bs.at[to], br.at[r], to, s)

    @loop(4)
    def _(m):
        part = pl.ds(pl.multiple_of(128 * m, 128), 128)
        acc = down(m, b)
        pair_copy(m).wait_recv()
        acc = acc + pair[part, :].astype(F32)
        ret_src[pl.ds(4 * m, 4)] = acc.astype(BF).reshape(4, 32, 512)
        for t in range(4):
            to = 4 * m + t

            @pl.when(to != r)
            def _():
                b_copy(to).start()

    ret[r] = ret_src[r]

    @loop(NR)
    def _(n):
        @pl.when(n != r)
        def _():
            remote(ret_src.at[0], ret.at[n], bs.at[0], br.at[n], n, s).wait_recv()

    total = dot(back[...], ret[...].reshape(512, 512))
    for t in range(NS):
        f_src[t] = total[4 * t : 4 * t + 4, :].astype(BF)

    def f_copy(d):
        to = rem(s + d, NS)
        return remote(f_src.at[to], fin.at[s], es.at[d], er.at[d], r, to)

    fin[s] = f_src[s]

    @loop(NS, 1)
    def _(d):
        f_copy(d).start()

    for e in range(1, NX):
        p_copy(e).wait_send()
        gu_copy(e).wait_send()
        hid_copy(e).wait_send()

    @loop(NY, 1)
    def _(d):
        y_copy(d).wait_send()

    @loop(4)
    def _(j):
        @pl.when(2 * j + top != y)
        def _():
            mid_copy(j).wait_send()

    @loop(NS, 1)
    def _(d):
        sq_copy(d).wait_send()
        a_copy(d).wait()

    @loop(NR, 1)
    def _(d):
        z_copy(d).wait_send()

    @loop(NR)
    def _(d):
        pass_copy(d).wait_send()

    @loop(4)
    def _(m):
        pair_copy(m).wait_send()

    @loop(NR)
    def _(n):
        @pl.when(n != r)
        def _():
            b_copy(n).wait_send()

    @loop(NS, 1)
    def _(d):
        f_copy(d).wait()

    for xx in range(NX):
        for bb in range(2):
            acc = fin[bb * NX + xx].astype(F32)
            for j in range(1, 4):
                acc = acc + fin[(2 * j + bb) * NX + xx].astype(F32)
            e_out[:, 1024 * xx + 512 * bb : 1024 * xx + 512 * bb + 512] = acc.astype(BF)


VM = pl.BlockSpec(memory_space=pltpu.VMEM)
HB = pl.BlockSpec(memory_space=pl.ANY)


def sds(shape, dtype=BF):
    return jax.ShapeDtypeStruct(shape, dtype)


def dma(*shape):
    return pltpu.SemaphoreType.DMA(shape)


def body(
    queries, kv_cache, tree_kv, context_lengths, tree_parents, resid, out_weight, norm_gain,
    expert_ids, gate_weights, w_gate, w_up, w_down,
):
    r, s, x, y = place()
    j = div(y, 2)
    b = rem(y, 2)
    h = rem(x, 2)
    q_in = queries[0].reshape(4, 2, 2048).transpose(1, 0, 2)
    both = jnp.concatenate([kv_cache[0], tree_kv[0], jnp.zeros((12, 2, 256), BF)], axis=0)
    kv_in = both.reshape(SPAN, 2, 2, 128).transpose(2, 1, 0, 3)
    res_in = resid[0].reshape(4, NX, NY, 128).transpose(2, 1, 0, 3).reshape(NS, 4, 128)
    parents = tree_parents[0]
    node = jnp.arange(128, dtype=jnp.int32)
    link = ((parents[None, :] == node[:, None]) | (node[:, None] == node[None, :])).astype(BF)
    q_out, kv_out, res_out, reach = pl.pallas_call(
        gather_kernel,
        name="gather",
        out_shape=(sds((NS, 4, 2048)), sds((2, 2, SPAN, 128)), sds((NS, 4, 128)), sds((128, 128))),
        in_specs=[VM] * 4,
        out_specs=(VM,) * 4,
        scratch_shapes=[
            pltpu.VMEM((NY, 2, 4, 2048), BF), pltpu.VMEM((128, 128), BF),
            dma(NY), dma(NY), dma(NY, NX), dma(NY, NX), dma(2), dma(NS), dma(NS), dma(3),
        ],
        compiler_params=pltpu.CompilerParams(collective_id=0, has_side_effects=True),
    )(q_in, kv_in, res_in, link)
    query = q_out.reshape(128, 2048)
    keys = kv_out[:, 0].reshape(KEYS, 128)
    vals = kv_out[:, 1].reshape(KEYS, 128).T
    base = s - h
    spot = jnp.arange(SPAN, dtype=jnp.int32)
    shard = base + jnp.arange(2, dtype=jnp.int32)[:, None]
    seen = (spot[None, :] < 512) & (shard * 512 + spot[None, :] < context_lengths[0])
    bias = jnp.where(seen, 0.0, MASKED).astype(F32)
    kin = lax.dynamic_slice_in_dim(reach, 4 * base, 8, 0).astype(F32).reshape(2, 4, 128)
    kin = jnp.where(kin > 0.5, 0.0, MASKED)
    bias = jnp.broadcast_to(bias[:, :, None], (2, SPAN, 128))
    bias = lax.dynamic_update_slice(bias, kin, (0, 512, 0)).reshape(KEYS, 128)
    ids, gates = expert_ids[0], gate_weights[0]
    mine = 4 * jnp.arange(16, dtype=jnp.int32) + j
    hit = ids[None] == mine[:, None, None]
    chosen = jnp.any(hit, axis=2)
    rate = jnp.sum(jnp.where(hit, gates[None].astype(F32), 0.0), axis=2)
    before = (node[:, None] < node[None, :]).astype(BF)
    slot = jnp.dot(chosen.astype(BF), before, preferred_element_type=F32)
    seats = jnp.arange(32, dtype=jnp.int32).astype(F32)
    seated = chosen[:, None, :] & (slot[:, None, :] == seats[None, :, None])
    sel = seated.astype(BF).reshape(512, 128)
    back = jnp.where(seated, rate[:, None, :], 0.0).astype(BF).reshape(512, 128).T
    gain = lax.dynamic_slice_in_dim(norm_gain, x * 1024 + b * 512, 512, 0).astype(F32).reshape(4, 1, 128)
    a_out, e_out = pl.pallas_call(
        main_kernel,
        name="layer",
        out_shape=(sds((NS, 4, 128)), sds((4, 4096))),
        in_specs=[VM] * 9 + [HB] * 3,
        out_specs=(VM, VM),
        scratch_shapes=[
            pltpu.VMEM((16, 128, 128), BF), pltpu.VMEM((16, 16, 128), F32),
            pltpu.VMEM((16, 128, 128), BF), pltpu.VMEM((16, 16, 128), F32),
            pltpu.VMEM((NX, 128, 1024), BF), pltpu.VMEM((NX, 128, 1024), BF),
            pltpu.VMEM((NY, 128, 128), BF), pltpu.VMEM((NY, 128, 128), BF),
            pltpu.VMEM((NS, 4, 128), BF), pltpu.VMEM((8, 128), F32), pltpu.VMEM((NS, 8, 128), F32),
            pltpu.VMEM((128, 128), BF), pltpu.VMEM((4, 128, 128), BF),
            pltpu.VMEM((16, 32, 512), BF), pltpu.VMEM((2, 16, 32, 512), BF),
            pltpu.VMEM((NX, 1024, 256), BF), pltpu.VMEM((NX, 128, 1024), BF),
            pltpu.VMEM((NX, 512, 256), BF), pltpu.VMEM((NX, 512, 256), BF),
            pltpu.VMEM((512, 128), BF), pltpu.VMEM((NX, 512, 128), BF),
            pltpu.VMEM((512, 512), BF), pltpu.VMEM((512, 512), BF),
            pltpu.VMEM((16, 32, 512), BF), pltpu.VMEM((16, 32, 512), BF),
            pltpu.VMEM((NS, 4, 512), BF), pltpu.VMEM((NS, 4, 512), BF),
            dma(16), dma(16), dma(16), dma(16), dma(4), dma(4), dma(8), dma(8),
            dma(NS), dma(NS), dma(NS), dma(NS), dma(4), dma(4), dma(16), dma(16), dma(16), dma(16),
            dma(4), dma(4), dma(4), dma(4), dma(4), dma(4), dma(4), dma(4), dma(4), dma(4),
            dma(4), dma(4), dma(16), dma(16), dma(NS), dma(NS), dma(6),
        ],
        compiler_params=pltpu.CompilerParams(collective_id=1, has_side_effects=True),
    )(
        query, keys, vals, bias, res_out.reshape(128, 128), out_weight, gain, sel, back,
        w_gate[0].reshape(NX, 1024, 128), w_up[0].reshape(NX, 1024, 128), w_down[0],
    )
    attended = a_out.reshape(NY, NX, 4, 128).transpose(2, 1, 0, 3).reshape(1, 4, 4096)
    return attended, e_out[None]


def solution(mesh):
    placed = (
        P("req", "seq", None),
        P("req", "seq", None, None),
        P("req", "seq", None, None),
        P("req"),
        P("req", None),
        P("req", "seq", None),
        P("seq", None),
        P(),
        P("req", None, None),
        P("req", None, None),
        P(("req", "seq"), None, None),
        P(("req", "seq"), None, None),
        P(("req", "seq"), None, None),
    )
    return jax.shard_map(
        body,
        mesh=mesh,
        in_specs=placed,
        out_specs=(P("req", "seq", None), P("req", "seq", None)),
        check_vma=False,
    )
```

```python
import jax
import jax.numpy as jnp
from jax import lax
from jax.experimental import pallas as pl
from jax.experimental.pallas import tpu as pltpu
from jax.sharding import PartitionSpec as P

BF = jnp.bfloat16
F32 = jnp.float32
MESH = pl.DeviceIdType.MESH
NX, NY = 4, 8
NR, NS = 16, 32
SPAN = 528
KEYS = 2 * SPAN
CHUNKS = 4
MASKED = -1e30
FLOOR = -1e29
EPS = 1e-06


def rem(a, b):
    return lax.rem(a, jnp.int32(b))


def div(a, b):
    return lax.div(a, jnp.int32(b))


def place():
    r = lax.axis_index("req")
    s = lax.axis_index("seq")
    return r, s, rem(s, NX), div(s, NX)


def remote(src, dst, send, recv, r, s):
    return pltpu.make_async_remote_copy(
        src_ref=src, dst_ref=dst, send_sem=send, recv_sem=recv, device_id=(r, s), device_id_type=MESH
    )


def loop(n, first=0):
    def run(fn):
        def step(i, c):
            fn(i)
            return c

        lax.fori_loop(first, n, step, 0)

    return run


def dot(a, b):
    return jnp.dot(a, b, preferred_element_type=F32)


def reach_of(o):
    half = div(o + 1, 2)
    return jnp.where(rem(o, 2) == 1, half, rem(NR - half, NR))


def lanes(first, size):
    return pl.ds(pl.multiple_of(first, 128), size)


def part_of(g):
    return slice(128 * g, 128 * g + 128)


def layer_kernel(
    q, k_in, vt_in, res, link, length, ids, gates, gain, w_out, w_gate, w_up, w_down,
    a_out, e_out,
    qy, q_got, qf, k, vt, bias, res_got, rf, reach, reach_f, chosen, rates, sel, back,
    out_src, st_src, got, got_st, p_src, p_got, y_src, y_got, a_src, sq_src, sq, mid_src, mid_q,
    d_src, rows, wgu, wd, gu_src, gu, hid_src, hid, pair_src, pair, ret_src, ret, f_src, fin,
    qys, qyr, qxs, qxr, ks, kr, rs, rr,
    hs, hr, ts, tr, ps, pr, ys, yr, as_, ar, qs, qr, ms, mr, zs, zr, fs, fr,
    gs, gr, us, ur, ds_, dr, gus, gur, hds, hdr, pas, par, bs, br, es, er, ls,
):
    r, s, x, y = place()
    h = rem(x, 2)
    b = rem(y, 2)
    j = div(y, 2)
    top = div(y, 4)
    mate = s + NX - 2 * NX * b
    twin = s + 1 - 2 * h
    number = y * 2 + div(x, 2)
    barrier = pltpu.get_barrier_semaphore()

    @loop(NS, 1)
    def _(d):
        pl.semaphore_signal(barrier, inc=1, device_id=(r, rem(s + d, NS)), device_id_type=MESH)

    @loop(NR, 1)
    def _(d):
        pl.semaphore_signal(barrier, inc=1, device_id=(rem(r + d, NR), s), device_id_type=MESH)

    def x_at(e):
        return rem(x + e, NX)

    def gate_copy(e, first=0, size=1024):
        to = x_at(e)
        span = pl.ds(first, size)
        return remote(w_gate.at[to, span], wgu.at[x, span, pl.ds(0, 128)], gs.at[e], gr.at[e], r, y * NX + to)

    def up_copy(e):
        to = x_at(e)
        return remote(w_up.at[to], wgu.at[x, :, pl.ds(128, 128)], us.at[e], ur.at[e], r, y * NX + to)

    def down_copy(e):
        to = x_at(e)
        return remote(w_down.at[:, lanes(to * 1024, 1024)], wd.at[x], ds_.at[e], dr.at[e], r, y * NX + to)

    own_g = pltpu.make_async_copy(w_gate.at[x], wgu.at[x, :, pl.ds(0, 128)], ls.at[0])
    own_u = pltpu.make_async_copy(w_up.at[x], wgu.at[x, :, pl.ds(128, 128)], ls.at[1])
    own_d = pltpu.make_async_copy(w_down.at[:, lanes(x * 1024, 1024)], wd.at[x], ls.at[2])
    own_g.start()
    own_u.start()
    own_d.start()

    def qy_copy(d):
        return remote(q, qy.at[y], qys.at[d], qyr.at[d], r, rem(y + d, NY) * NX + x)

    def qx_copy(d, e):
        row = rem(y + NY - d, NY)
        to = x_at(e)
        cols = lanes(rem(to, 2) * 2048, 2048)
        return remote(qy.at[row, :, cols], q_got.at[row * NX + x], qxs.at[d, e], qxr.at[d, e], r, y * NX + to)

    def first_copy(e):
        to = x_at(e)
        cols = lanes(rem(to, 2) * 2048, 2048)
        return remote(q.at[:, cols], q_got.at[y * NX + x], qxs.at[0, e], qxr.at[0, e], r, y * NX + to)

    def k_copy():
        return remote(k_in.at[1 - h], k.at[h], ks.at[0], kr.at[0], r, twin)

    def v_copy():
        return remote(vt_in.at[1 - h], vt.at[h], ks.at[1], kr.at[1], r, twin)

    def column(to):
        return lanes(rem(to, NX) * 1024 + div(to, NX) * 128, 128)

    def res_copy(d):
        to = rem(s + d, NS)
        return remote(res.at[:, column(to)], res_got.at[s], rs.at[d], rr.at[d], r, to)

    pl.semaphore_wait(barrier, NS + NR - 2)

    @loop(NY, 1)
    def _(d):
        qy_copy(d).start()

    for e in (2, 1, 3):
        first_copy(e).start()
    k_copy().start()
    v_copy().start()
    mine_q = lanes(h * 2048, 2048)
    q_got[s] = q[:, mine_q]
    k[h] = k_in[h]
    vt[h] = vt_in[h]
    res_got[s] = res[:, column(s)]

    for o in range(NR):
        expert = (4 * rem(r + reach_of(jnp.int32(o)), NR) + j).astype(F32)
        hit = ids[...] == expert
        chosen[o : o + 1, :] = jnp.sum(jnp.where(hit, 1.0, 0.0), axis=0, keepdims=True)
        rates[o : o + 1, :] = jnp.sum(jnp.where(hit, gates[...], 0.0), axis=0, keepdims=True)

    @loop(NY, 1)
    def _(d):
        qy_copy(d).wait_recv()
        for e in (2, 1, 3):
            qx_copy(d, e).start()
        row = rem(y + NY - d, NY)
        q_got[row * NX + x] = qy[row, :, mine_q]

    @loop(NS, 1)
    def _(d):
        res_copy(d).start()

    reach[...] = link[...]

    @loop(5)
    def _(i):
        reach[...] = jnp.minimum(dot(reach[...], reach[...]), 1.0).astype(BF)

    reach_f[...] = jnp.where(reach[...].astype(F32) > 0.5, 0.0, MASKED)
    kin = reach_f[pl.ds(pl.multiple_of(8 * div(s, 2), 8), 8), :]
    spot = lax.broadcasted_iota(jnp.int32, (SPAN, 128), 0)
    for p in range(2):
        first = ((s - h + p) * 512).astype(F32)
        seen = (spot < 512) & (spot.astype(F32) + first < length[...])
        bias[p * SPAN : (p + 1) * SPAN, :] = jnp.where(seen, 0.0, MASKED)
        bias[p * SPAN + 512 : p * SPAN + 516, :] = kin[4 * p : 4 * p + 4, :]

    earlier = lax.broadcasted_iota(jnp.int32, (128, 128), 0) < lax.broadcasted_iota(jnp.int32, (128, 128), 1)
    slot = dot(chosen[...].astype(BF), jnp.where(earlier, 1.0, 0.0).astype(BF))
    seat = lax.broadcasted_iota(jnp.int32, (32, 128), 0).astype(F32)
    for g in range(CHUNKS):
        tall = []
        for o in range(4 * g, 4 * g + 4):
            hit = (slot[o : o + 1, :] == seat) & (chosen[o : o + 1, :] > 0.5)
            tall.append(jnp.where(hit, rates[o : o + 1, :], 0.0))
            sel[32 * o : 32 * o + 32, :] = jnp.where(hit, 1.0, 0.0).astype(BF)
        back[:, part_of(g)] = jnp.transpose(jnp.concatenate(tall, axis=0)).astype(BF)

    k_copy().wait()
    v_copy().wait()
    for e in range(1, NX):
        first_copy(e).wait()

    @loop(NY, 1)
    def _(d):
        qy_copy(d).wait_send()
        for e in range(1, NX):
            qx_copy(d, e).wait()

    for t in range(NS):
        qf[4 * t : 4 * t + 4, :] = q_got[t].astype(F32)

    def out_copy(i):
        return remote(out_src.at[i], got.at[number], hs.at[i], hr.at[number], r, 16 * h + i)

    def st_copy(i):
        return remote(st_src.at[i], got_st.at[number], ts.at[i], tr.at[number], r, 16 * h + i)

    def head_at(n):
        return rem(n + number, 16)

    def send_head(i):
        @pl.when(16 * h + i != s)
        def _():
            out_copy(i).start()
            st_copy(i).start()

        @pl.when(16 * h + i == s)
        def _():
            got[number] = out_src[i]
            got_st[number] = st_src[i]

    @loop(16)
    def _(n):
        i = head_at(n)
        heads = qf[:, lanes(i * 128, 128)].astype(BF)
        score = lax.dot_general(
            k[...].reshape(KEYS, 128), heads, (((1,), (1,)), ((), ())), preferred_element_type=F32
        )
        score = score * (128 ** (-0.5)) + bias[...]
        peak = jnp.maximum(jnp.max(score, axis=0, keepdims=True), FLOOR)
        prob = jnp.exp(score - peak)
        total = jnp.sum(prob, axis=0, keepdims=True)
        prob = prob.astype(BF)
        out_src[i] = (dot(vt[0], prob[:SPAN]) + dot(vt[1], prob[SPAN:])).astype(BF)
        st_src[i] = jnp.concatenate([jnp.broadcast_to(peak, (8, 128)), jnp.broadcast_to(total, (8, 128))], axis=0)

        @pl.when(n >= 1)
        def _():
            send_head(head_at(n + 15))

        for e in (1, 3):
            gate_copy(jnp.int32(e), pl.multiple_of(64 * n, 64), 64).start()

    send_head(head_at(jnp.int32(15)))
    gate_copy(jnp.int32(2)).start()

    @loop(NS, 1)
    def _(d):
        res_copy(d).wait()

    for t in range(NS):
        rf[4 * t : 4 * t + 4, :] = res_got[t].astype(F32)

    @loop(16)
    def _(n):
        who = div(n, 2) * NX + 2 * rem(n, 2) + top

        @pl.when(who != s)
        def _():
            remote(out_src.at[0], got.at[n], hs.at[0], hr.at[n], r, who).wait_recv()
            remote(st_src.at[0], got_st.at[n], ts.at[0], tr.at[n], r, who).wait_recv()

    peaks = got_st[:, 0:1, :]
    totals = got_st[:, 8:9, :]
    peak = jnp.max(peaks, axis=0)
    factor = jnp.exp(peaks - peak[None])
    denom = jnp.sum(factor * totals, axis=0)
    numer = jnp.zeros((128, 128), F32)
    for n in range(16):
        numer = numer + factor[n] * got[n].astype(F32)
    att = jnp.transpose(numer / denom).astype(BF)

    def p_copy(e):
        return remote(p_src.at[e], p_got.at[e], ps.at[e], pr.at[e], r, y * NX + x_at(e))

    for e in (2, 1, 3, 0):
        p_src[e] = dot(att, w_out[:, lanes(x_at(jnp.int32(e)) * 1024, 1024)]).astype(BF)
        if e:
            p_copy(e).start()
    for e in (2, 1, 3):
        up_copy(jnp.int32(e)).start()
    for e in (2, 1, 3):
        down_copy(jnp.int32(e)).start()
    for e in range(1, NX):
        p_copy(e).wait_recv()

    def y_copy(d):
        to = rem(y + d, NY)
        return remote(y_src.at[to], y_got.at[d], ys.at[d], yr.at[d], r, to * NX + x)

    for t in range(NY):
        acc = p_src[0, :, part_of(t)].astype(F32)
        for e in range(1, NX):
            acc = acc + p_got[e, :, part_of(t)].astype(F32)
        y_src[t] = acc.astype(BF)

    @loop(NY, 1)
    def _(d):
        y_copy(d).start()

    acc = y_src[y].astype(F32)
    for d in range(1, NY):
        y_copy(jnp.int32(d)).wait_recv()
        acc = acc + y_got[d].astype(F32)
    attended = acc.astype(BF)
    wide = attended.astype(F32)
    mid = (rf[...] + wide).astype(BF)
    midf = mid.astype(F32)
    mid_src[...] = mid
    col = jnp.sum(midf * midf, axis=1, keepdims=True)
    sq_src[...] = jnp.transpose(jnp.broadcast_to(col, (128, 128)))[0:8, :]
    sq[s] = sq_src[...]

    def mid_copy(n):
        to = (2 * n + top) * NX + x
        return remote(mid_src, mid_q.at[rem(y, 4)], ms.at[n], mr.at[rem(y, 4)], r, to)

    def sq_copy(d):
        return remote(sq_src, sq.at[s], qs.at[d], qr.at[d], r, rem(s + d, NS))

    def a_copy(d):
        to = rem(s + d, NS)
        return remote(a_src.at[to], a_out.at[:, column(s)], as_.at[d], ar.at[d], r, to)

    @loop(NS, 1)
    def _(d):
        sq_copy(d).start()

    @loop(4)
    def _(n):
        @pl.when(2 * n + top != y)
        def _():
            mid_copy(n).start()

        @pl.when(2 * n + top == y)
        def _():
            mid_q[rem(y, 4)] = mid_src[...]

    for t in range(NS):
        a_src[t] = wide[4 * t : 4 * t + 4, :].astype(BF)
    a_out[:, column(s)] = a_src[s]

    @loop(NS, 1)
    def _(d):
        a_copy(d).start()

    @loop(4)
    def _(t):
        @pl.when(4 * b + t != y)
        def _():
            remote(mid_src, mid_q.at[t], ms.at[0], mr.at[t], r, (4 * b + t) * NX + x).wait_recv()

    @loop(NS, 1)
    def _(d):
        sq_copy(d).wait_recv()

    square = jnp.sum(sq[:, 0:1, :], axis=0)
    scale = lax.rsqrt(square * (1.0 / 4096.0) + EPS)
    scale = jnp.transpose(jnp.broadcast_to(scale, (128, 128)))
    half = x * 2 + b

    def z_copy(o):
        to = rem(r + reach_of(o), NR)
        return remote(d_src.at[o], rows.at[b, o], zs.at[o], zr.at[o], to, s)

    def pass_copy(o):
        return remote(rows.at[b, o], rows.at[b, o], fs.at[o], fr.at[o], r, mate)

    def pass_got(o):
        return remote(rows.at[1 - b, o], rows.at[1 - b, o], fs.at[o], fr.at[o], r, mate)

    normed = jnp.concatenate(
        [(mid_q[t].astype(F32) * scale * gain[half, t]).astype(BF) for t in range(4)], axis=1
    )
    for g in range(CHUNKS):
        d_src[4 * g : 4 * g + 4] = dot(sel[part_of(g), :], normed).astype(BF).reshape(4, 32, 512)
        for o in range(max(4 * g, 1), 4 * g + 4):
            z_copy(jnp.int32(o)).start()
    rows[b, 0] = d_src[0]
    pass_copy(jnp.int32(0)).start()

    def gu_copy(e, g):
        return remote(
            gu_src.at[e, pl.ds(128 * g, 128)], gu.at[e, pl.ds(128 * g, 128)], gus.at[e, g], gur.at[e, g],
            r, y * NX + x_at(e),
        )

    def hid_copy(e, g):
        return remote(
            hid_src.at[pl.ds(128 * g, 128)], hid.at[x, pl.ds(128 * g, 128)], hds.at[e, g], hdr.at[e, g],
            r, y * NX + x_at(e),
        )

    def pair_copy(g):
        span = pl.ds(128 * g, 128)
        return remote(pair_src.at[span], pair.at[span], pas.at[g], par.at[g], r, mate)

    def b_copy(o):
        to = rem(r + NR - reach_of(o), NR)
        return remote(ret_src.at[o], ret.at[o], bs.at[o], br.at[o], to, s)

    def forward(g):
        for o in range(max(4 * g, 1), 4 * g + 4):
            z_copy(jnp.int32(o)).wait_recv()
            pass_copy(jnp.int32(o)).start()

    def gate_up(g):
        if g == 0:
            own_g.wait()
            own_u.wait()
            for e in range(1, NX):
                gate_copy(jnp.int32(e)).wait()
                up_copy(jnp.int32(e)).wait()
        for o in range(4 * g, 4 * g + 4):
            pass_got(jnp.int32(o)).wait_recv()
        left = rows[0, 4 * g : 4 * g + 4].reshape(128, 512)
        right = rows[1, 4 * g : 4 * g + 4].reshape(128, 512)
        for e in (2, 1, 3, 0):
            to = x_at(jnp.int32(e))
            gu_src[e, part_of(g), :] = (dot(left, wgu[to, 0:512, :]) + dot(right, wgu[to, 512:1024, :])).astype(BF)
            if e:
                gu_copy(e, g).start()

    def hidden(g):
        acc = gu_src[0, part_of(g), :].astype(F32)
        for e in range(1, NX):
            gu_copy(e, g).wait_recv()
            acc = acc + gu[e, part_of(g), :].astype(F32)
        gate = acc[:, 0:128]
        hid_src[part_of(g), :] = (gate / (1.0 + jnp.exp(-gate)) * acc[:, 128:256]).astype(BF)
        for e in (2, 1, 3):
            hid_copy(e, g).start()
        hid[x, part_of(g), :] = hid_src[part_of(g), :]

    def product(g, side):
        cols = lanes(side * 512, 512)
        acc = dot(hid[0, part_of(g), :], wd[0, :, cols])
        for t in range(1, NX):
            acc = acc + dot(hid[t, part_of(g), :], wd[t, :, cols])
        return acc

    def down(g):
        if g == 0:
            own_d.wait()
            for e in range(1, NX):
                down_copy(jnp.int32(e)).wait()
        for e in range(1, NX):
            hid_copy(e, g).wait_recv()
        pair_src[part_of(g), :] = product(g, 1 - b).astype(BF)
        pair_copy(g).start()

    def give(g):
        acc = product(g, b)
        pair_copy(g).wait_recv()
        acc = acc + pair[part_of(g), :].astype(F32)
        ret_src[4 * g : 4 * g + 4] = acc.astype(BF).reshape(4, 32, 512)
        for o in range(max(4 * g, 1), 4 * g + 4):
            b_copy(jnp.int32(o)).start()
        if g == 0:
            ret[0] = ret_src[0]

    forward(0)
    forward(1)
    gate_up(0)
    forward(2)
    gate_up(1)
    forward(3)
    gate_up(2)
    hidden(0)
    gate_up(3)
    hidden(1)
    down(0)
    hidden(2)
    down(1)
    give(0)
    hidden(3)
    down(2)
    give(1)
    down(3)
    give(2)
    give(3)

    total = jnp.zeros((128, 512), F32)
    for g in range(CHUNKS):
        for o in range(max(4 * g, 1), 4 * g + 4):
            b_copy(jnp.int32(o)).wait_recv()
        total = total + dot(back[:, part_of(g)], ret[4 * g : 4 * g + 4].reshape(128, 512))
    for t in range(NS):
        f_src[t] = total[4 * t : 4 * t + 4, :].astype(BF)

    def f_copy(d):
        to = rem(s + d, NS)
        return remote(f_src.at[to], fin.at[s], es.at[d], er.at[d], r, to)

    fin[s] = f_src[s]

    @loop(NS, 1)
    def _(d):
        f_copy(d).start()

    @loop(16)
    def _(i):
        @pl.when(16 * h + i != s)
        def _():
            out_copy(i).wait_send()
            st_copy(i).wait_send()

    for e in range(1, NX):
        p_copy(e).wait_send()
        for g in range(CHUNKS):
            gu_copy(e, g).wait_send()
            hid_copy(e, g).wait_send()

    @loop(NY, 1)
    def _(d):
        y_copy(d).wait_send()

    @loop(4)
    def _(n):
        @pl.when(2 * n + top != y)
        def _():
            mid_copy(n).wait_send()

    @loop(NS, 1)
    def _(d):
        sq_copy(d).wait_send()
        a_copy(d).wait()

    @loop(NR, 1)
    def _(o):
        z_copy(o).wait_send()
        b_copy(o).wait_send()

    @loop(NR)
    def _(o):
        pass_copy(o).wait_send()

    for g in range(CHUNKS):
        pair_copy(g).wait_send()

    @loop(NS, 1)
    def _(d):
        f_copy(d).wait()

    for xx in range(NX):
        for bb in range(2):
            acc = fin[bb * NX + xx].astype(F32)
            for n in range(1, 4):
                acc = acc + fin[(2 * n + bb) * NX + xx].astype(F32)
            e_out[:, 1024 * xx + 512 * bb : 1024 * xx + 512 * bb + 512] = acc.astype(BF)


VM = pl.BlockSpec(memory_space=pltpu.VMEM)
HB = pl.BlockSpec(memory_space=pl.ANY)


def sds(shape, dtype=BF):
    return jax.ShapeDtypeStruct(shape, dtype)


def dma(*shape):
    return pltpu.SemaphoreType.DMA(shape)


def vm(*shape, dtype=BF):
    return pltpu.VMEM(shape, dtype)


def body(
    queries, kv_cache, tree_kv, context_lengths, tree_parents, resid, out_weight, norm_gain,
    expert_ids, gate_weights, w_gate, w_up, w_down,
):
    both = jnp.concatenate([kv_cache[0], tree_kv[0], jnp.zeros((12, 2, 256), BF)], axis=0)
    k_in = both[:, 0].reshape(SPAN, 2, 128).transpose(1, 0, 2)
    vt_in = both[:, 1].reshape(SPAN, 2, 128).transpose(1, 2, 0)
    parents = tree_parents[0]
    node = jnp.arange(128, dtype=jnp.int32)
    link = ((parents[None, :] == node[:, None]) | (node[:, None] == node[None, :])).astype(BF)
    length = jnp.broadcast_to(context_lengths.astype(F32)[:, None], (1, 128))
    gain = norm_gain.astype(F32).reshape(8, 4, 1, 128)
    a_out, e_out = pl.pallas_call(
        layer_kernel,
        name="layer",
        out_shape=(sds((4, 4096)), sds((4, 4096))),
        in_specs=[VM] * 10 + [HB] * 3,
        out_specs=(VM, VM),
        scratch_shapes=[
            vm(NY, 4, 4096), vm(NS, 4, 2048), vm(128, 2048, dtype=F32), vm(2, SPAN, 128), vm(2, 128, SPAN),
            vm(KEYS, 128, dtype=F32), vm(NS, 4, 128), vm(128, 128, dtype=F32), vm(128, 128),
            vm(128, 128, dtype=F32), vm(NR, 128, dtype=F32), vm(NR, 128, dtype=F32), vm(512, 128), vm(128, 512),
            vm(16, 128, 128), vm(16, 16, 128, dtype=F32), vm(16, 128, 128), vm(16, 16, 128, dtype=F32),
            vm(NX, 128, 1024), vm(NX, 128, 1024), vm(NY, 128, 128), vm(NY, 128, 128),
            vm(NS, 4, 128), vm(8, 128, dtype=F32), vm(NS, 8, 128, dtype=F32), vm(128, 128), vm(4, 128, 128),
            vm(16, 32, 512), vm(2, 16, 32, 512), vm(NX, 1024, 256), vm(NX, 128, 1024),
            vm(NX, 512, 256), vm(NX, 512, 256), vm(512, 128), vm(NX, 512, 128), vm(512, 512), vm(512, 512),
            vm(16, 32, 512), vm(16, 32, 512), vm(NS, 4, 512), vm(NS, 4, 512),
            dma(NY), dma(NY), dma(NY, NX), dma(NY, NX), dma(2), dma(2), dma(NS), dma(NS),
            dma(16), dma(16), dma(16), dma(16), dma(4), dma(4), dma(NY), dma(NY),
            dma(NS), dma(NS), dma(NS), dma(NS), dma(4), dma(4), dma(NR), dma(NR), dma(NR), dma(NR),
            dma(4), dma(4), dma(4), dma(4), dma(4), dma(4), dma(NX, CHUNKS), dma(NX, CHUNKS),
            dma(NX, CHUNKS), dma(NX, CHUNKS), dma(CHUNKS), dma(CHUNKS), dma(NR), dma(NR), dma(NS), dma(NS), dma(3),
        ],
        compiler_params=pltpu.CompilerParams(collective_id=0, has_side_effects=True),
    )(
        queries[0], k_in, vt_in, resid[0], link, length,
        expert_ids[0].T.astype(F32), gate_weights[0].T.astype(F32), gain, out_weight,
        w_gate[0].reshape(NX, 1024, 128), w_up[0].reshape(NX, 1024, 128), w_down[0],
    )
    return a_out[None], e_out[None]


def solution(mesh):
    placed = (
        P("req", "seq", None),
        P("req", "seq", None, None),
        P("req", "seq", None, None),
        P("req"),
        P("req", None),
        P("req", "seq", None),
        P("seq", None),
        P(),
        P("req", None, None),
        P("req", None, None),
        P(("req", "seq"), None, None),
        P(("req", "seq"), None, None),
        P(("req", "seq"), None, None),
    )
    return jax.shard_map(
        body,
        mesh=mesh,
        in_specs=placed,
        out_specs=(P("req", "seq", None), P("req", "seq", None)),
        check_vma=False,
    )
```

```python
import jax
import jax.numpy as jnp
from jax import lax
from jax.experimental import pallas as pl
from jax.experimental.pallas import tpu as pltpu
from jax.sharding import PartitionSpec as P

BF = jnp.bfloat16
F32 = jnp.float32
MESH = pl.DeviceIdType.MESH
NX, NY = 4, 8
NR, NS = 16, 32
SPAN = 528
KEYS = 2 * SPAN
CHUNKS = 4
MASKED = -1e30
FLOOR = -1e29
EPS = 1e-06


def rem(a, b):
    return lax.rem(a, jnp.int32(b))


def div(a, b):
    return lax.div(a, jnp.int32(b))


def place():
    r = lax.axis_index("req")
    s = lax.axis_index("seq")
    return r, s, rem(s, NX), div(s, NX)


def remote(src, dst, send, recv, r, s):
    return pltpu.make_async_remote_copy(
        src_ref=src, dst_ref=dst, send_sem=send, recv_sem=recv, device_id=(r, s), device_id_type=MESH
    )


def loop(n, first=0):
    def run(fn):
        def step(i, c):
            fn(i)
            return c

        lax.fori_loop(first, n, step, 0)

    return run


def dot(a, b):
    return jnp.dot(a, b, preferred_element_type=F32)


def spread_of(o, n):
    o = n - 1 - o
    half = div(o + 1, 2)
    return jnp.where(rem(o, 2) == 1, half, rem(n - half, n))


def reach_of(o):
    return spread_of(o, NR)


FAR = (4, 3, 5, 2, 6, 1, 7, 0)


def lanes(first, size):
    return pl.ds(pl.multiple_of(first, 128), size)


def part_of(g):
    return slice(128 * g, 128 * g + 128)


def layer_kernel(
    q, kv_in, tree_in, res, parents, length, ids, gates, gain, w_out, w_gate, w_up, w_down,
    a_out, e_out,
    qy, q_got, qf, k, v, vt, bias, res_got, rf, reach, reach_f, chosen, rates, sel, back,
    out_src, st_src, got, got_st, p_src, p_got, y_src, y_got, a_src, sq_src, sq, mid_src, mid_q,
    d_src, rows, wgu, wd, gu_src, gu, hid_src, hid, pair_src, pair, ret_src, ret, f_src, fin,
    qys, qyr, qxs, qxr, ks, kr, rs, rr,
    hs, hr, ts, tr, ps, pr, ys, yr, as_, ar, qs, qr, ms, mr, zs, zr, fs, fr,
    gs, gr, us, ur, ds_, dr, gus, gur, hds, hdr, pas, par, bs, br, es, er, ls,
):
    r, s, x, y = place()
    h = rem(x, 2)
    b = rem(y, 2)
    j = div(y, 2)
    top = div(y, 4)
    mate = s + NX - 2 * NX * b
    twin = s + 1 - 2 * h
    number = y * 2 + div(x, 2)
    barrier = pltpu.get_barrier_semaphore()

    @loop(NS, 1)
    def _(d):
        pl.semaphore_signal(barrier, inc=1, device_id=(r, rem(s + d, NS)), device_id_type=MESH)

    @loop(NR, 1)
    def _(d):
        pl.semaphore_signal(barrier, inc=1, device_id=(rem(r + d, NR), s), device_id_type=MESH)

    def x_at(e):
        return rem(x + e, NX)

    def gate_copy(e, first=0, size=1024):
        to = x_at(e)
        span = pl.ds(first, size)
        return remote(w_gate.at[to, span], wgu.at[x, span, pl.ds(0, 128)], gs.at[e], gr.at[e], r, y * NX + to)

    def up_copy(e):
        to = x_at(e)
        return remote(w_up.at[to], wgu.at[x, :, pl.ds(128, 128)], us.at[e], ur.at[e], r, y * NX + to)

    def down_copy(e):
        to = x_at(e)
        return remote(w_down.at[:, lanes(to * 1024, 1024)], wd.at[x], ds_.at[e], dr.at[e], r, y * NX + to)

    own_g = pltpu.make_async_copy(w_gate.at[x], wgu.at[x, :, pl.ds(0, 128)], ls.at[0])
    own_u = pltpu.make_async_copy(w_up.at[x], wgu.at[x, :, pl.ds(128, 128)], ls.at[1])
    own_d = pltpu.make_async_copy(w_down.at[:, lanes(x * 1024, 1024)], wd.at[x], ls.at[2])
    own_g.start()
    own_u.start()
    own_d.start()

    def qy_copy(d):
        return remote(q, qy.at[y], qys.at[d], qyr.at[d], r, rem(y + spread_of(d, NY), NY) * NX + x)

    def qx_copy(d, e):
        row = rem(y + NY - spread_of(d, NY), NY)
        to = x_at(e)
        cols = lanes(rem(to, 2) * 2048, 2048)
        return remote(qy.at[row, :, cols], q_got.at[row * NX + x], qxs.at[d, e], qxr.at[d, e], r, y * NX + to)

    def first_copy(e):
        to = x_at(e)
        cols = lanes(rem(to, 2) * 2048, 2048)
        return remote(q.at[:, cols], q_got.at[y * NX + x], qxs.at[NY - 1, e], qxr.at[NY - 1, e], r, y * NX + to)

    def kv_copies():
        ctx, new = pl.ds(0, 512), pl.ds(512, 16)
        return (
            remote(kv_in.at[1 - h], k.at[h, ctx], ks.at[0], kr.at[0], r, twin),
            remote(kv_in.at[3 - h], v.at[h, ctx], ks.at[1], kr.at[1], r, twin),
            remote(tree_in.at[1 - h], k.at[h, new], ks.at[2], kr.at[2], r, twin),
            remote(tree_in.at[3 - h], v.at[h, new], ks.at[3], kr.at[3], r, twin),
        )

    def column(to):
        return lanes(rem(to, NX) * 1024 + div(to, NX) * 128, 128)

    def res_copy(d):
        to = rem(s + spread_of(d, NS), NS)
        return remote(res.at[:, column(to)], res_got.at[s], rs.at[d], rr.at[d], r, to)

    pl.semaphore_wait(barrier, NS + NR - 2)

    @loop(NY - 1)
    def _(d):
        qy_copy(d).start()

    for e in (2, 1, 3):
        first_copy(e).start()
    for copy in kv_copies():
        copy.start()
    mine_q = lanes(h * 2048, 2048)
    q_got[s] = q[:, mine_q]
    k[h, 0:512] = kv_in[h]
    k[h, 512:528] = tree_in[h]
    v[h, 0:512] = kv_in[2 + h]
    v[h, 512:528] = tree_in[2 + h]
    res_got[s] = res[:, column(s)]

    for o in range(NR):
        hit = ids[...] == 4 * rem(r + reach_of(jnp.int32(o)), NR) + j
        chosen[o : o + 1, :] = jnp.sum(jnp.where(hit, 1.0, 0.0), axis=0, keepdims=True)
        rates[o : o + 1, :] = jnp.sum(jnp.where(hit, gates[...].astype(F32), 0.0), axis=0, keepdims=True)

    @loop(NY - 1)
    def _(d):
        qy_copy(d).wait_recv()
        for e in (2, 1, 3):
            qx_copy(d, e).start()
        row = rem(y + NY - spread_of(d, NY), NY)
        q_got[row * NX + x] = qy[row, :, mine_q]

    @loop(NS - 1)
    def _(d):
        res_copy(d).start()

    node = lax.broadcasted_iota(jnp.int32, (128, 128), 0)
    spot = lax.broadcasted_iota(jnp.int32, (128, 128), 1)
    reach[...] = jnp.where((parents[...] == node) | (node == spot), 1.0, 0.0).astype(BF)

    @loop(5)
    def _(i):
        reach[...] = jnp.minimum(dot(reach[...], reach[...]), 1.0).astype(BF)

    reach_f[...] = jnp.where(reach[...].astype(F32) > 0.5, 0.0, MASKED)
    kin = reach_f[pl.ds(pl.multiple_of(8 * div(s, 2), 8), 8), :]
    spot = lax.broadcasted_iota(jnp.int32, (SPAN, 128), 0)
    for p in range(2):
        first = (s - h + p) * 512
        seen = (spot < 512) & (spot + first < length[0])
        bias[p * SPAN : (p + 1) * SPAN, :] = jnp.where(seen, 0.0, MASKED)
        bias[p * SPAN + 512 : p * SPAN + 516, :] = kin[4 * p : 4 * p + 4, :]

    earlier = lax.broadcasted_iota(jnp.int32, (128, 128), 0) < lax.broadcasted_iota(jnp.int32, (128, 128), 1)
    slot = dot(chosen[...].astype(BF), jnp.where(earlier, 1.0, 0.0).astype(BF))
    seat = lax.broadcasted_iota(jnp.int32, (32, 128), 0).astype(F32)
    for g in range(CHUNKS):
        tall = []
        for o in range(4 * g, 4 * g + 4):
            hit = (slot[o : o + 1, :] == seat) & (chosen[o : o + 1, :] > 0.5)
            tall.append(jnp.where(hit, rates[o : o + 1, :], 0.0))
            sel[32 * o : 32 * o + 32, :] = jnp.where(hit, 1.0, 0.0).astype(BF)
        back[:, part_of(g)] = jnp.transpose(jnp.concatenate(tall, axis=0)).astype(BF)

    for copy in kv_copies():
        copy.wait()
    for p in range(2):
        for t in range(4):
            vt[p, :, part_of(t)] = jnp.transpose(v[p, part_of(t), :].astype(F32)).astype(BF)
        last = jnp.concatenate([v[p, 512:528, :].astype(F32), jnp.zeros((112, 128), F32)], axis=0)
        vt[p, :, 512:528] = jnp.transpose(last)[:, 0:16].astype(BF)
    for e in range(1, NX):
        first_copy(e).wait()

    @loop(NY - 1)
    def _(d):
        qy_copy(d).wait_send()
        for e in range(1, NX):
            qx_copy(d, e).wait()

    for t in range(NS):
        qf[4 * t : 4 * t + 4, :] = q_got[t].astype(F32)

    def out_copy(i):
        return remote(out_src.at[i], got.at[number], hs.at[i], hr.at[number], r, 16 * h + i)

    def st_copy(i):
        return remote(st_src.at[i], got_st.at[number], ts.at[i], tr.at[number], r, 16 * h + i)

    def head_at(n):
        return rem(n + number, 16)

    def send_head(i):
        @pl.when(16 * h + i != s)
        def _():
            out_copy(i).start()
            st_copy(i).start()

        @pl.when(16 * h + i == s)
        def _():
            got[number] = out_src[i]
            got_st[number] = st_src[i]

    @loop(16)
    def _(n):
        i = head_at(n)
        heads = qf[:, lanes(i * 128, 128)].astype(BF)
        score = lax.dot_general(
            k[...].reshape(KEYS, 128), heads, (((1,), (1,)), ((), ())), preferred_element_type=F32
        )
        score = score * (128 ** (-0.5)) + bias[...]
        peak = jnp.maximum(jnp.max(score, axis=0, keepdims=True), FLOOR)
        prob = jnp.exp(score - peak)
        total = jnp.sum(prob, axis=0, keepdims=True)
        prob = prob.astype(BF)
        out_src[i] = (dot(vt[0], prob[:SPAN]) + dot(vt[1], prob[SPAN:])).astype(BF)
        st_src[i] = jnp.concatenate([peak, total], axis=0)

        @pl.when(n >= 1)
        def _():
            send_head(head_at(n + 15))

        for e in (1, 3):
            gate_copy(jnp.int32(e), pl.multiple_of(64 * n, 64), 64).start()

    send_head(head_at(jnp.int32(15)))
    gate_copy(jnp.int32(2)).start()

    @loop(NS - 1)
    def _(d):
        res_copy(d).wait()

    for t in range(NS):
        rf[4 * t : 4 * t + 4, :] = res_got[t].astype(F32)

    @loop(16)
    def _(n):
        who = div(n, 2) * NX + 2 * rem(n, 2) + top

        @pl.when(who != s)
        def _():
            remote(out_src.at[0], got.at[n], hs.at[0], hr.at[n], r, who).wait_recv()
            remote(st_src.at[0], got_st.at[n], ts.at[0], tr.at[n], r, who).wait_recv()

    peaks = got_st[:, 0:1, :]
    totals = got_st[:, 1:2, :]
    peak = jnp.max(peaks, axis=0)
    factor = jnp.exp(peaks - peak[None])
    denom = jnp.sum(factor * totals, axis=0)
    numer = jnp.zeros((128, 128), F32)
    for n in range(16):
        numer = numer + factor[n] * got[n].astype(F32)
    att = jnp.transpose(numer / denom).astype(BF)

    def p_copy(e, n):
        t = rem(y + FAR[n], NY)
        return remote(p_src.at[e, t], p_got.at[e, t], ps.at[e, n], pr.at[e, n], r, y * NX + x_at(e))

    for n in range(NY):
        t = rem(y + FAR[n], NY)
        for e in (2, 1, 3, 0):
            cols = lanes(x_at(jnp.int32(e)) * 1024 + t * 128, 128)
            p_src[e, t] = dot(att, w_out[:, cols]).astype(BF)
            if e:
                p_copy(e, n).start()
    for e in (2, 1, 3):
        up_copy(jnp.int32(e)).start()
    for e in (2, 1, 3):
        down_copy(jnp.int32(e)).start()

    def y_copy(n):
        to = rem(y + FAR[n], NY)
        return remote(y_src.at[n], y_got.at[n], ys.at[n], yr.at[n], r, to * NX + x)

    for n in range(NY):
        t = rem(y + FAR[n], NY)
        acc = p_src[0, t].astype(F32)
        for e in range(1, NX):
            p_copy(e, n).wait_recv()
            acc = acc + p_got[e, t].astype(F32)
        if FAR[n]:
            y_src[n] = acc.astype(BF)
            y_copy(n).start()
    for n in range(NY - 1):
        y_copy(n).wait_recv()
        acc = acc + y_got[n].astype(F32)
    attended = acc.astype(BF)
    wide = attended.astype(F32)
    mid = (rf[...] + wide).astype(BF)
    midf = mid.astype(F32)
    mid_src[...] = mid
    col = jnp.sum(midf * midf, axis=1, keepdims=True)
    sq_src[...] = jnp.transpose(jnp.broadcast_to(col, (128, 128)))[0:1, :]
    sq[s] = sq_src[...]

    def mid_copy(n):
        to = (2 * n + top) * NX + x
        return remote(mid_src, mid_q.at[rem(y, 4)], ms.at[n], mr.at[rem(y, 4)], r, to)

    def sq_copy(d):
        return remote(sq_src, sq.at[s], qs.at[d], qr.at[d], r, rem(s + spread_of(d, NS), NS))

    def a_copy(d):
        to = rem(s + spread_of(d, NS), NS)
        return remote(a_src.at[to], a_out.at[:, column(s)], as_.at[d], ar.at[d], r, to)

    @loop(NS - 1)
    def _(d):
        sq_copy(d).start()

    @loop(4)
    def _(n):
        @pl.when(2 * n + top != y)
        def _():
            mid_copy(n).start()

        @pl.when(2 * n + top == y)
        def _():
            mid_q[rem(y, 4)] = mid_src[...]

    for t in range(NS):
        a_src[t] = wide[4 * t : 4 * t + 4, :].astype(BF)
    a_out[:, column(s)] = a_src[s]

    @loop(NS - 1)
    def _(d):
        a_copy(d).start()

    @loop(4)
    def _(t):
        @pl.when(4 * b + t != y)
        def _():
            remote(mid_src, mid_q.at[t], ms.at[0], mr.at[t], r, (4 * b + t) * NX + x).wait_recv()

    @loop(NS - 1)
    def _(d):
        sq_copy(d).wait_recv()

    square = jnp.sum(sq[...], axis=0)
    scale = lax.rsqrt(square * (1.0 / 4096.0) + EPS)
    scale = jnp.transpose(jnp.broadcast_to(scale, (128, 128)))
    half = x * 2 + b

    def z_copy(o):
        to = rem(r + reach_of(o), NR)
        return remote(d_src.at[o], rows.at[b, o], zs.at[o], zr.at[o], to, s)

    def pass_copy(o):
        return remote(rows.at[b, o], rows.at[b, o], fs.at[o], fr.at[o], r, mate)

    def pass_got(o):
        return remote(rows.at[1 - b, o], rows.at[1 - b, o], fs.at[o], fr.at[o], r, mate)

    normed = jnp.concatenate(
        [
            (mid_q[t].astype(F32) * scale * gain[:, lanes(half * 512 + 128 * t, 128)].astype(F32)).astype(BF)
            for t in range(4)
        ], axis=1
    )
    for g in range(CHUNKS):
        d_src[4 * g : 4 * g + 4] = dot(sel[part_of(g), :], normed).astype(BF).reshape(4, 32, 512)
        for o in range(4 * g, min(4 * g + 4, NR - 1)):
            z_copy(jnp.int32(o)).start()
    rows[b, NR - 1] = d_src[NR - 1]
    pass_copy(jnp.int32(NR - 1)).start()

    def gu_copy(e, g):
        return remote(
            gu_src.at[e, pl.ds(128 * g, 128)], gu.at[e, pl.ds(128 * g, 128)], gus.at[e, g], gur.at[e, g],
            r, y * NX + x_at(e),
        )

    def hid_copy(e, g):
        return remote(
            hid_src.at[pl.ds(128 * g, 128)], hid.at[x, pl.ds(128 * g, 128)], hds.at[e, g], hdr.at[e, g],
            r, y * NX + x_at(e),
        )

    def pair_copy(g):
        span = pl.ds(128 * g, 128)
        return remote(pair_src.at[span], pair.at[span], pas.at[g], par.at[g], r, mate)

    def b_copy(o):
        to = rem(r + NR - reach_of(o), NR)
        return remote(ret_src.at[o], ret.at[o], bs.at[o], br.at[o], to, s)

    def forward(g):
        for o in range(4 * g, min(4 * g + 4, NR - 1)):
            z_copy(jnp.int32(o)).wait_recv()
            pass_copy(jnp.int32(o)).start()

    def gate_up(g):
        if g == 0:
            own_g.wait()
            own_u.wait()
            for e in range(1, NX):
                gate_copy(jnp.int32(e)).wait()
                up_copy(jnp.int32(e)).wait()
        for o in range(4 * g, 4 * g + 4):
            pass_got(jnp.int32(o)).wait_recv()
        left = rows[0, 4 * g : 4 * g + 4].reshape(128, 512)
        right = rows[1, 4 * g : 4 * g + 4].reshape(128, 512)
        for e in (2, 1, 3, 0):
            to = x_at(jnp.int32(e))
            gu_src[e, part_of(g), :] = (dot(left, wgu[to, 0:512, :]) + dot(right, wgu[to, 512:1024, :])).astype(BF)
            if e:
                gu_copy(e, g).start()

    def hidden(g):
        acc = gu_src[0, part_of(g), :].astype(F32)
        for e in range(1, NX):
            gu_copy(e, g).wait_recv()
            acc = acc + gu[e, part_of(g), :].astype(F32)
        gate = acc[:, 0:128]
        hid_src[part_of(g), :] = (gate / (1.0 + jnp.exp(-gate)) * acc[:, 128:256]).astype(BF)
        for e in (2, 1, 3):
            hid_copy(e, g).start()
        hid[x, part_of(g), :] = hid_src[part_of(g), :]

    def product(g, side):
        cols = lanes(side * 512, 512)
        acc = dot(hid[0, part_of(g), :], wd[0, :, cols])
        for t in range(1, NX):
            acc = acc + dot(hid[t, part_of(g), :], wd[t, :, cols])
        return acc

    def down(g):
        if g == 0:
            own_d.wait()
            for e in range(1, NX):
                down_copy(jnp.int32(e)).wait()
        for e in range(1, NX):
            hid_copy(e, g).wait_recv()
        pair_src[part_of(g), :] = product(g, 1 - b).astype(BF)
        pair_copy(g).start()

    def give(g):
        acc = product(g, b)
        pair_copy(g).wait_recv()
        acc = acc + pair[part_of(g), :].astype(F32)
        ret_src[4 * g : 4 * g + 4] = acc.astype(BF).reshape(4, 32, 512)
        for o in range(4 * g, min(4 * g + 4, NR - 1)):
            b_copy(jnp.int32(o)).start()
        if g == CHUNKS - 1:
            ret[NR - 1] = ret_src[NR - 1]

    forward(0)
    forward(1)
    gate_up(0)
    forward(2)
    gate_up(1)
    forward(3)
    gate_up(2)
    hidden(0)
    gate_up(3)
    hidden(1)
    down(0)
    hidden(2)
    down(1)
    give(0)
    hidden(3)
    down(2)
    give(1)
    down(3)
    give(2)
    give(3)

    total = jnp.zeros((128, 512), F32)
    for g in range(CHUNKS):
        for o in range(4 * g, min(4 * g + 4, NR - 1)):
            b_copy(jnp.int32(o)).wait_recv()
        total = total + dot(back[:, part_of(g)], ret[4 * g : 4 * g + 4].reshape(128, 512))
    for t in range(NS):
        f_src[t] = total[4 * t : 4 * t + 4, :].astype(BF)

    def f_copy(d):
        to = rem(s + spread_of(d, NS), NS)
        return remote(f_src.at[to], fin.at[s], es.at[d], er.at[d], r, to)

    fin[s] = f_src[s]

    @loop(NS - 1)
    def _(d):
        f_copy(d).start()

    @loop(16)
    def _(i):
        @pl.when(16 * h + i != s)
        def _():
            out_copy(i).wait_send()
            st_copy(i).wait_send()

    for e in range(1, NX):
        for n in range(NY):
            p_copy(e, n).wait_send()
        for g in range(CHUNKS):
            gu_copy(e, g).wait_send()
            hid_copy(e, g).wait_send()

    for n in range(NY - 1):
        y_copy(n).wait_send()

    @loop(4)
    def _(n):
        @pl.when(2 * n + top != y)
        def _():
            mid_copy(n).wait_send()

    @loop(NS - 1)
    def _(d):
        sq_copy(d).wait_send()
        a_copy(d).wait()

    @loop(NR - 1)
    def _(o):
        z_copy(o).wait_send()
        b_copy(o).wait_send()

    @loop(NR)
    def _(o):
        pass_copy(o).wait_send()

    for g in range(CHUNKS):
        pair_copy(g).wait_send()

    @loop(NS - 1)
    def _(d):
        f_copy(d).wait()

    for xx in range(NX):
        for bb in range(2):
            acc = fin[bb * NX + xx].astype(F32)
            for n in range(1, 4):
                acc = acc + fin[(2 * n + bb) * NX + xx].astype(F32)
            e_out[:, 1024 * xx + 512 * bb : 1024 * xx + 512 * bb + 512] = acc.astype(BF)


VM = pl.BlockSpec(memory_space=pltpu.VMEM)
HB = pl.BlockSpec(memory_space=pl.ANY)


def sds(shape, dtype=BF):
    return jax.ShapeDtypeStruct(shape, dtype)


def dma(*shape):
    return pltpu.SemaphoreType.DMA(shape)


def vm(*shape, dtype=BF):
    return pltpu.VMEM(shape, dtype)


def body(
    queries, kv_cache, tree_kv, context_lengths, tree_parents, resid, out_weight, norm_gain,
    expert_ids, gate_weights, w_gate, w_up, w_down,
):
    kv_in = kv_cache[0].reshape(512, 4, 128).transpose(1, 0, 2)
    tree_in = jnp.pad(tree_kv[0].reshape(4, 4, 128).transpose(1, 0, 2), ((0, 0), (0, 12), (0, 0)))
    a_out, e_out = pl.pallas_call(
        layer_kernel,
        name="layer",
        out_shape=(sds((4, 4096)), sds((4, 4096))),
        in_specs=[VM] * 5 + [pl.BlockSpec(memory_space=pltpu.SMEM)] + [VM] * 4 + [HB] * 3,
        out_specs=(VM, VM),
        scratch_shapes=[
            vm(NY, 4, 4096), vm(NS, 4, 2048), vm(128, 2048, dtype=F32), vm(2, SPAN, 128), vm(2, SPAN, 128), vm(2, 128, SPAN),
            vm(KEYS, 128, dtype=F32), vm(NS, 4, 128), vm(128, 128, dtype=F32), vm(128, 128),
            vm(128, 128, dtype=F32), vm(NR, 128, dtype=F32), vm(NR, 128, dtype=F32), vm(512, 128), vm(128, 512),
            vm(16, 128, 128), vm(16, 2, 128, dtype=F32), vm(16, 128, 128), vm(16, 2, 128, dtype=F32),
            vm(NX, NY, 128, 128), vm(NX, NY, 128, 128), vm(NY, 128, 128), vm(NY, 128, 128),
            vm(NS, 4, 128), vm(1, 128, dtype=F32), vm(NS, 1, 128, dtype=F32), vm(128, 128), vm(4, 128, 128),
            vm(16, 32, 512), vm(2, 16, 32, 512), vm(NX, 1024, 256), vm(NX, 128, 1024),
            vm(NX, 512, 256), vm(NX, 512, 256), vm(512, 128), vm(NX, 512, 128), vm(512, 512), vm(512, 512),
            vm(16, 32, 512), vm(16, 32, 512), vm(NS, 4, 512), vm(NS, 4, 512),
            dma(NY), dma(NY), dma(NY, NX), dma(NY, NX), dma(4), dma(4), dma(NS), dma(NS),
            dma(16), dma(16), dma(16), dma(16), dma(NX, NY), dma(NX, NY), dma(NY), dma(NY),
            dma(NS), dma(NS), dma(NS), dma(NS), dma(4), dma(4), dma(NR), dma(NR), dma(NR), dma(NR),
            dma(4), dma(4), dma(4), dma(4), dma(4), dma(4), dma(NX, CHUNKS), dma(NX, CHUNKS),
            dma(NX, CHUNKS), dma(NX, CHUNKS), dma(CHUNKS), dma(CHUNKS), dma(NR), dma(NR), dma(NS), dma(NS), dma(3),
        ],
        compiler_params=pltpu.CompilerParams(collective_id=0, has_side_effects=True),
    )(
        queries[0], kv_in, tree_in, resid[0], tree_parents, context_lengths,
        expert_ids[0].T, gate_weights[0].T, norm_gain.reshape(1, 4096), out_weight,
        w_gate[0].reshape(NX, 1024, 128), w_up[0].reshape(NX, 1024, 128), w_down[0],
    )
    return a_out[None], e_out[None]


def solution(mesh):
    placed = (
        P("req", "seq", None),
        P("req", "seq", None, None),
        P("req", "seq", None, None),
        P("req"),
        P("req", None),
        P("req", "seq", None),
        P("seq", None),
        P(),
        P("req", None, None),
        P("req", None, None),
        P(("req", "seq"), None, None),
        P(("req", "seq"), None, None),
        P(("req", "seq"), None, None),
    )
    return jax.shard_map(
        body,
        mesh=mesh,
        in_specs=placed,
        out_specs=(P("req", "seq", None), P("req", "seq", None)),
        check_vma=False,
    )
```

```python
import math

import jax
import jax.numpy as jnp
from jax import lax
from jax.experimental import pallas as pl
from jax.experimental.pallas import tpu as pltpu
from jax.sharding import PartitionSpec as P

BF = jnp.bfloat16
F32 = jnp.float32
MESH = pl.DeviceIdType.MESH
NX, NY = 4, 8
NR, NS = 16, 32
SPAN = 528
KEYS = 2 * SPAN
CHUNKS = 4
TEMPER = 128 ** (-0.5) * math.log2(math.e)
MASKED = -1e30
FLOOR = -1e29
EPS = 1e-06


def rem(a, b):
    return lax.rem(a, jnp.int32(b))


def div(a, b):
    return lax.div(a, jnp.int32(b))


def place():
    r = lax.axis_index("req")
    s = lax.axis_index("seq")
    return r, s, rem(s, NX), div(s, NX)


def remote(src, dst, send, recv, r, s):
    return pltpu.make_async_remote_copy(
        src_ref=src, dst_ref=dst, send_sem=send, recv_sem=recv, device_id=(r, s), device_id_type=MESH
    )


def loop(n, first=0):
    def run(fn):
        def step(i, c):
            fn(i)
            return c

        lax.fori_loop(first, n, step, 0)

    return run


def dot(a, b):
    return jnp.dot(a, b, preferred_element_type=F32)


def spread_of(o, n):
    o = n - 1 - o
    half = div(o + 1, 2)
    return jnp.where(rem(o, 2) == 1, half, rem(n - half, n))


def reach_of(o):
    return spread_of(o, NR)


FAR = (4, 3, 5, 2, 6, 1, 7, 0)


def lanes(first, size):
    return pl.ds(pl.multiple_of(first, 128), size)


def part_of(g):
    return slice(128 * g, 128 * g + 128)


def layer_kernel(
    q, kv_in, tree_in, res, parents, length, ids, gates, gain, w_out, w_gate, w_up, w_down,
    a_out, e_out,
    qy, q_got, qf, k, v, vt, bias, res_got, rf, reach, reach_f, chosen, rates, sel, back,
    out_src, st_src, got, got_st, p_src, p_got, y_src, y_got, a_src, sq_src, sq, mid_src, mid_q,
    d_src, rows, wgu, wd, gu_src, gu, hid_src, hid, pair_src, pair, ret_src, ret, f_src, fin,
    qys, qyr, qxs, qxr, ks, kr, rs, rr,
    hs, hr, ts, tr, ps, pr, ys, yr, as_, ar, qs, qr, ms, mr, zs, zr, fs, fr,
    gs, gr, us, ur, ds_, dr, gus, gur, hds, hdr, pas, par, bs, br, es, er, ls,
):
    r, s, x, y = place()
    b = rem(y, 2)
    h = b
    j = div(y, 2)
    top = div(y, 4)
    mate = s + NX - 2 * NX * b
    number = div(y, 2) * NX + x
    barrier = pltpu.get_barrier_semaphore()

    @loop(NS, 1)
    def _(d):
        pl.semaphore_signal(barrier, inc=1, device_id=(r, rem(s + d, NS)), device_id_type=MESH)

    @loop(NR, 1)
    def _(d):
        pl.semaphore_signal(barrier, inc=1, device_id=(rem(r + d, NR), s), device_id_type=MESH)

    def x_at(e):
        return rem(x + e, NX)

    def gate_copy(e, first=0, size=1024):
        to = x_at(e)
        span = pl.ds(first, size)
        return remote(w_gate.at[to, span], wgu.at[x, span, pl.ds(0, 128)], gs.at[e], gr.at[e], r, y * NX + to)

    def up_copy(e):
        to = x_at(e)
        return remote(w_up.at[to], wgu.at[x, :, pl.ds(128, 128)], us.at[e], ur.at[e], r, y * NX + to)

    def down_copy(e):
        to = x_at(e)
        return remote(w_down.at[:, lanes(to * 1024, 1024)], wd.at[x], ds_.at[e], dr.at[e], r, y * NX + to)

    own_g = pltpu.make_async_copy(w_gate.at[x], wgu.at[x, :, pl.ds(0, 128)], ls.at[0])
    own_u = pltpu.make_async_copy(w_up.at[x], wgu.at[x, :, pl.ds(128, 128)], ls.at[1])
    own_d = pltpu.make_async_copy(w_down.at[:, lanes(x * 1024, 1024)], wd.at[x], ls.at[2])
    own_g.start()
    own_u.start()
    own_d.start()

    mine_q = lanes(h * 2048, 2048)

    def qy_copy(d):
        to = rem(y + spread_of(d, NY), NY)
        return remote(q.at[:, lanes(rem(to, 2) * 2048, 2048)], qy.at[y], qys.at[d], qyr.at[d], r, to * NX + x)

    def qx_copy(d, e):
        row = rem(y + NY - spread_of(d, NY), NY)
        return remote(qy.at[row], q_got.at[row * NX + x], qxs.at[d, e], qxr.at[d, e], r, y * NX + x_at(e))

    def first_copy(e):
        return remote(q.at[:, mine_q], q_got.at[s], qxs.at[NY - 1, e], qxr.at[NY - 1, e], r, y * NX + x_at(e))

    def kv_copies():
        ctx, new = pl.ds(0, 512), pl.ds(512, 16)
        return (
            remote(kv_in.at[1 - h], k.at[h, ctx], ks.at[0], kr.at[0], r, mate),
            remote(kv_in.at[3 - h], v.at[h, ctx], ks.at[1], kr.at[1], r, mate),
            remote(tree_in.at[1 - h], k.at[h, new], ks.at[2], kr.at[2], r, mate),
            remote(tree_in.at[3 - h], v.at[h, new], ks.at[3], kr.at[3], r, mate),
        )

    def column(to):
        return lanes(rem(to, NX) * 1024 + div(to, NX) * 128, 128)

    def res_copy(d):
        to = rem(s + spread_of(d, NS), NS)
        return remote(res.at[:, column(to)], res_got.at[s], rs.at[d], rr.at[d], r, to)

    pl.semaphore_wait(barrier, NS + NR - 2)

    @loop(NY - 1)
    def _(d):
        qy_copy(d).start()

    for e in (2, 1, 3):
        first_copy(e).start()
    for copy in kv_copies():
        copy.start()
    q_got[s] = q[:, mine_q]
    k[h, 0:512] = kv_in[h]
    k[h, 512:528] = tree_in[h]
    v[h, 0:512] = kv_in[2 + h]
    v[h, 512:528] = tree_in[2 + h]
    res_got[s] = res[:, column(s)]

    for o in range(NR):
        hit = ids[...] == 4 * rem(r + reach_of(jnp.int32(o)), NR) + j
        chosen[o : o + 1, :] = jnp.sum(jnp.where(hit, 1.0, 0.0), axis=0, keepdims=True)
        rates[o : o + 1, :] = jnp.sum(jnp.where(hit, gates[...].astype(F32), 0.0), axis=0, keepdims=True)

    @loop(NY - 1)
    def _(d):
        qy_copy(d).wait_recv()
        for e in (2, 1, 3):
            qx_copy(d, e).start()
        row = rem(y + NY - spread_of(d, NY), NY)
        q_got[row * NX + x] = qy[row]

    @loop(NS - 1)
    def _(d):
        res_copy(d).start()

    node = lax.broadcasted_iota(jnp.int32, (128, 128), 0)
    spot = lax.broadcasted_iota(jnp.int32, (128, 128), 1)
    reach[...] = jnp.where((parents[...] == node) | (node == spot), 1.0, 0.0).astype(BF)

    @loop(5)
    def _(i):
        reach[...] = jnp.minimum(dot(reach[...], reach[...]), 1.0).astype(BF)

    reach_f[...] = jnp.where(reach[...].astype(F32) > 0.5, 0.0, MASKED)
    base = s - NX * h
    spot = lax.broadcasted_iota(jnp.int32, (SPAN, 128), 0)
    for p in range(2):
        first = (base + NX * p) * 512
        eight = reach_f[pl.ds(pl.multiple_of(8 * (div(base, 2) + 2 * p), 8), 8), :]
        seen = (spot < 512) & (spot + first < length[0])
        bias[p * SPAN : (p + 1) * SPAN, :] = jnp.where(seen, 0.0, MASKED)
        bias[p * SPAN + 512 : p * SPAN + 516, :] = jnp.where(rem(base, 2) == 1, eight[4:8, :], eight[0:4, :])

    earlier = lax.broadcasted_iota(jnp.int32, (128, 128), 0) < lax.broadcasted_iota(jnp.int32, (128, 128), 1)
    slot = dot(chosen[...].astype(BF), jnp.where(earlier, 1.0, 0.0).astype(BF))
    seat = lax.broadcasted_iota(jnp.int32, (32, 128), 0).astype(F32)
    for g in range(CHUNKS):
        tall = []
        for o in range(4 * g, 4 * g + 4):
            hit = (slot[o : o + 1, :] == seat) & (chosen[o : o + 1, :] > 0.5)
            tall.append(jnp.where(hit, rates[o : o + 1, :], 0.0))
            sel[32 * o : 32 * o + 32, :] = jnp.where(hit, 1.0, 0.0).astype(BF)
        back[:, part_of(g)] = jnp.transpose(jnp.concatenate(tall, axis=0)).astype(BF)

    for copy in kv_copies():
        copy.wait()
    for p in range(2):
        for t in range(4):
            vt[p, :, part_of(t)] = jnp.transpose(v[p, part_of(t), :].astype(F32)).astype(BF)
        last = jnp.concatenate([v[p, 512:528, :].astype(F32), jnp.zeros((112, 128), F32)], axis=0)
        vt[p, :, 512:528] = jnp.transpose(last)[:, 0:16].astype(BF)
    for e in range(1, NX):
        first_copy(e).wait()

    @loop(NY - 1)
    def _(d):
        qy_copy(d).wait_send()
        for e in range(1, NX):
            qx_copy(d, e).wait()

    for t in range(NS):
        qf[4 * t : 4 * t + 4, :] = q_got[t].astype(F32)

    def out_copy(i):
        return remote(out_src.at[i], got.at[number], hs.at[i], hr.at[number], r, 16 * h + i)

    def st_copy(i):
        return remote(st_src.at[i], got_st.at[number], ts.at[i], tr.at[number], r, 16 * h + i)

    def head_at(n):
        return rem(n + number, 16)

    def send_head(i):
        @pl.when(16 * h + i != s)
        def _():
            out_copy(i).start()
            st_copy(i).start()

        @pl.when(16 * h + i == s)
        def _():
            got[number] = out_src[i]
            got_st[number] = st_src[i]

    @loop(16)
    def _(n):
        i = head_at(n)
        heads = qf[:, lanes(i * 128, 128)].astype(BF)
        score = lax.dot_general(
            k[...].reshape(KEYS, 128), heads, (((1,), (1,)), ((), ())), preferred_element_type=F32
        )
        score = score + bias[...]
        peak = jnp.maximum(jnp.max(score, axis=0, keepdims=True), FLOOR)
        prob = jnp.exp2((score - peak) * TEMPER)
        total = jnp.sum(prob, axis=0, keepdims=True)
        prob = prob.astype(BF)
        out_src[i] = (dot(vt[0], prob[:SPAN]) + dot(vt[1], prob[SPAN:])).astype(BF)
        st_src[i] = jnp.concatenate([peak, total], axis=0)

        @pl.when(n >= 1)
        def _():
            send_head(head_at(n + 15))

        for e in (1, 3):
            gate_copy(jnp.int32(e), pl.multiple_of(64 * n, 64), 64).start()

    send_head(head_at(jnp.int32(15)))
    gate_copy(jnp.int32(2)).start()

    @loop(NS - 1)
    def _(d):
        res_copy(d).wait()

    for t in range(NS):
        rf[4 * t : 4 * t + 4, :] = res_got[t].astype(F32)

    @loop(16)
    def _(n):
        who = (2 * div(n, NX) + top) * NX + rem(n, NX)

        @pl.when(who != s)
        def _():
            remote(out_src.at[0], got.at[n], hs.at[0], hr.at[n], r, who).wait_recv()
            remote(st_src.at[0], got_st.at[n], ts.at[0], tr.at[n], r, who).wait_recv()

    peaks = got_st[:, 0:1, :]
    totals = got_st[:, 1:2, :]
    peak = jnp.max(peaks, axis=0)
    factor = jnp.exp2((peaks - peak[None]) * TEMPER)
    denom = jnp.sum(factor * totals, axis=0)
    numer = jnp.zeros((128, 128), F32)
    for n in range(16):
        numer = numer + factor[n] * got[n].astype(F32)
    att = jnp.transpose(numer / denom).astype(BF)

    def p_copy(e, n):
        t = rem(y + FAR[n], NY)
        return remote(p_src.at[e, t], p_got.at[e, t], ps.at[e, n], pr.at[e, n], r, y * NX + x_at(e))

    for e in (2, 1, 3, 0):
        block = dot(att, w_out[:, lanes(x_at(jnp.int32(e)) * 1024, 1024)]).astype(BF)
        for t in range(NY):
            p_src[e, t] = block[:, part_of(t)]
    for n in range(NY):
        for e in (2, 1, 3):
            p_copy(e, n).start()

    def y_copy(n):
        to = rem(y + FAR[n], NY)
        return remote(y_src.at[n], y_got.at[n], ys.at[n], yr.at[n], r, to * NX + x)

    for n in range(NY):
        t = rem(y + FAR[n], NY)
        acc = p_src[0, t].astype(F32)
        for e in range(1, NX):
            p_copy(e, n).wait_recv()
            acc = acc + p_got[e, t].astype(F32)
        if FAR[n]:
            y_src[n] = acc.astype(BF)
            y_copy(n).start()
    for n in range(NY - 1):
        y_copy(n).wait_recv()
        acc = acc + y_got[n].astype(F32)
    attended = acc.astype(BF)
    wide = attended.astype(F32)
    mid = (rf[...] + wide).astype(BF)
    midf = mid.astype(F32)
    mid_src[...] = mid
    col = jnp.sum(midf * midf, axis=1, keepdims=True)
    sq_src[...] = jnp.transpose(jnp.broadcast_to(col, (128, 128)))[0:1, :]
    sq[s] = sq_src[...]

    def mid_copy(n):
        to = (2 * n + top) * NX + x
        return remote(mid_src, mid_q.at[rem(y, 4)], ms.at[n], mr.at[rem(y, 4)], r, to)

    def sq_copy(d):
        return remote(sq_src, sq.at[s], qs.at[d], qr.at[d], r, rem(s + spread_of(d, NS), NS))

    def a_copy(d):
        to = rem(s + spread_of(d, NS), NS)
        return remote(a_src.at[to], a_out.at[:, column(s)], as_.at[d], ar.at[d], r, to)

    @loop(NS - 1)
    def _(d):
        sq_copy(d).start()

    @loop(4)
    def _(n):
        @pl.when(2 * n + top != y)
        def _():
            mid_copy(n).start()

        @pl.when(2 * n + top == y)
        def _():
            mid_q[rem(y, 4)] = mid_src[...]

    for t in range(NS):
        a_src[t] = wide[4 * t : 4 * t + 4, :].astype(BF)
    a_out[:, column(s)] = a_src[s]

    @loop(NS - 1)
    def _(d):
        a_copy(d).start()

    for e in (2, 1, 3):
        up_copy(jnp.int32(e)).start()
    for e in (2, 1, 3):
        down_copy(jnp.int32(e)).start()

    @loop(4)
    def _(t):
        @pl.when(4 * b + t != y)
        def _():
            remote(mid_src, mid_q.at[t], ms.at[0], mr.at[t], r, (4 * b + t) * NX + x).wait_recv()

    @loop(NS - 1)
    def _(d):
        sq_copy(d).wait_recv()

    square = jnp.sum(sq[...], axis=0)
    scale = lax.rsqrt(square * (1.0 / 4096.0) + EPS)
    scale = jnp.transpose(jnp.broadcast_to(scale, (128, 128)))
    half = x * 2 + b

    def z_copy(o):
        to = rem(r + reach_of(o), NR)
        return remote(d_src.at[o], rows.at[b, o], zs.at[o], zr.at[o], to, s)

    def pass_copy(o):
        return remote(rows.at[b, o], rows.at[b, o], fs.at[o], fr.at[o], r, mate)

    def pass_got(o):
        return remote(rows.at[1 - b, o], rows.at[1 - b, o], fs.at[o], fr.at[o], r, mate)

    normed = jnp.concatenate(
        [
            (mid_q[t].astype(F32) * scale * gain[:, lanes(half * 512 + 128 * t, 128)].astype(F32)).astype(BF)
            for t in range(4)
        ], axis=1
    )
    for g in range(CHUNKS):
        d_src[4 * g : 4 * g + 4] = dot(sel[part_of(g), :], normed).astype(BF).reshape(4, 32, 512)
        for o in range(4 * g, min(4 * g + 4, NR - 1)):
            z_copy(jnp.int32(o)).start()
    rows[b, NR - 1] = d_src[NR - 1]
    pass_copy(jnp.int32(NR - 1)).start()

    def gu_copy(e, g):
        return remote(
            gu_src.at[e, pl.ds(128 * g, 128)], gu.at[e, pl.ds(128 * g, 128)], gus.at[e, g], gur.at[e, g],
            r, y * NX + x_at(e),
        )

    def hid_copy(e, g):
        return remote(
            hid_src.at[pl.ds(128 * g, 128)], hid.at[x, pl.ds(128 * g, 128)], hds.at[e, g], hdr.at[e, g],
            r, y * NX + x_at(e),
        )

    def pair_copy(g):
        span = pl.ds(128 * g, 128)
        return remote(pair_src.at[span], pair.at[span], pas.at[g], par.at[g], r, mate)

    def b_copy(o):
        to = rem(r + NR - reach_of(o), NR)
        return remote(ret_src.at[o], ret.at[o], bs.at[o], br.at[o], to, s)

    def forward(g):
        for o in range(4 * g, min(4 * g + 4, NR - 1)):
            z_copy(jnp.int32(o)).wait_recv()
            pass_copy(jnp.int32(o)).start()

    def gate_up(g):
        if g == 0:
            own_g.wait()
            own_u.wait()
            for e in range(1, NX):
                gate_copy(jnp.int32(e)).wait()
                up_copy(jnp.int32(e)).wait()
        for o in range(4 * g, 4 * g + 4):
            pass_got(jnp.int32(o)).wait_recv()
        left = rows[0, 4 * g : 4 * g + 4].reshape(128, 512)
        right = rows[1, 4 * g : 4 * g + 4].reshape(128, 512)
        for e in (2, 1, 3, 0):
            to = x_at(jnp.int32(e))
            gu_src[e, part_of(g), :] = (dot(left, wgu[to, 0:512, :]) + dot(right, wgu[to, 512:1024, :])).astype(BF)
            if e:
                gu_copy(e, g).start()

    def hidden(g):
        acc = gu_src[0, part_of(g), :].astype(F32)
        for e in range(1, NX):
            gu_copy(e, g).wait_recv()
            acc = acc + gu[e, part_of(g), :].astype(F32)
        gate = acc[:, 0:128]
        hid_src[part_of(g), :] = (gate / (1.0 + jnp.exp(-gate)) * acc[:, 128:256]).astype(BF)
        for e in (2, 1, 3):
            hid_copy(e, g).start()
        hid[x, part_of(g), :] = hid_src[part_of(g), :]

    def product(g, side):
        cols = lanes(side * 512, 512)
        acc = dot(hid[0, part_of(g), :], wd[0, :, cols])
        for t in range(1, NX):
            acc = acc + dot(hid[t, part_of(g), :], wd[t, :, cols])
        return acc

    def down(g):
        if g == 0:
            own_d.wait()
            for e in range(1, NX):
                down_copy(jnp.int32(e)).wait()
        for e in range(1, NX):
            hid_copy(e, g).wait_recv()
        pair_src[part_of(g), :] = product(g, 1 - b).astype(BF)
        pair_copy(g).start()

    def give(g):
        acc = product(g, b)
        pair_copy(g).wait_recv()
        acc = acc + pair[part_of(g), :].astype(F32)
        ret_src[4 * g : 4 * g + 4] = acc.astype(BF).reshape(4, 32, 512)
        for o in range(4 * g, min(4 * g + 4, NR - 1)):
            b_copy(jnp.int32(o)).start()
        if g == CHUNKS - 1:
            ret[NR - 1] = ret_src[NR - 1]

    forward(0)
    forward(1)
    gate_up(0)
    forward(2)
    gate_up(1)
    forward(3)
    gate_up(2)
    hidden(0)
    gate_up(3)
    hidden(1)
    down(0)
    hidden(2)
    down(1)
    give(0)
    hidden(3)
    down(2)
    give(1)
    down(3)
    give(2)
    give(3)

    total = jnp.zeros((128, 512), F32)
    for g in range(CHUNKS):
        for o in range(4 * g, min(4 * g + 4, NR - 1)):
            b_copy(jnp.int32(o)).wait_recv()
        total = total + dot(back[:, part_of(g)], ret[4 * g : 4 * g + 4].reshape(128, 512))
    for t in range(NS):
        f_src[t] = total[4 * t : 4 * t + 4, :].astype(BF)

    def f_copy(d):
        to = rem(s + spread_of(d, NS), NS)
        return remote(f_src.at[to], fin.at[s], es.at[d], er.at[d], r, to)

    fin[s] = f_src[s]

    @loop(NS - 1)
    def _(d):
        f_copy(d).start()

    @loop(16)
    def _(i):
        @pl.when(16 * h + i != s)
        def _():
            out_copy(i).wait_send()
            st_copy(i).wait_send()

    for e in range(1, NX):
        for n in range(NY):
            p_copy(e, n).wait_send()
        for g in range(CHUNKS):
            gu_copy(e, g).wait_send()
            hid_copy(e, g).wait_send()

    for n in range(NY - 1):
        y_copy(n).wait_send()

    @loop(4)
    def _(n):
        @pl.when(2 * n + top != y)
        def _():
            mid_copy(n).wait_send()

    @loop(NS - 1)
    def _(d):
        sq_copy(d).wait_send()
        a_copy(d).wait()

    @loop(NR - 1)
    def _(o):
        z_copy(o).wait_send()
        b_copy(o).wait_send()

    @loop(NR)
    def _(o):
        pass_copy(o).wait_send()

    for g in range(CHUNKS):
        pair_copy(g).wait_send()

    @loop(NS - 1)
    def _(d):
        f_copy(d).wait()

    for xx in range(NX):
        for bb in range(2):
            acc = fin[bb * NX + xx].astype(F32)
            for n in range(1, 4):
                acc = acc + fin[(2 * n + bb) * NX + xx].astype(F32)
            e_out[:, 1024 * xx + 512 * bb : 1024 * xx + 512 * bb + 512] = acc.astype(BF)


VM = pl.BlockSpec(memory_space=pltpu.VMEM)
HB = pl.BlockSpec(memory_space=pl.ANY)


def sds(shape, dtype=BF):
    return jax.ShapeDtypeStruct(shape, dtype)


def dma(*shape):
    return pltpu.SemaphoreType.DMA(shape)


def vm(*shape, dtype=BF):
    return pltpu.VMEM(shape, dtype)


def body(
    queries, kv_cache, tree_kv, context_lengths, tree_parents, resid, out_weight, norm_gain,
    expert_ids, gate_weights, w_gate, w_up, w_down,
):
    kv_in = kv_cache[0].reshape(512, 4, 128).transpose(1, 0, 2)
    tree_in = jnp.pad(tree_kv[0].reshape(4, 4, 128).transpose(1, 0, 2), ((0, 0), (0, 12), (0, 0)))
    a_out, e_out = pl.pallas_call(
        layer_kernel,
        name="layer",
        out_shape=(sds((4, 4096)), sds((4, 4096))),
        in_specs=[VM] * 5 + [pl.BlockSpec(memory_space=pltpu.SMEM)] + [VM] * 4 + [HB] * 3,
        out_specs=(VM, VM),
        scratch_shapes=[
            vm(NY, 4, 2048), vm(NS, 4, 2048), vm(128, 2048, dtype=F32), vm(2, SPAN, 128), vm(2, SPAN, 128), vm(2, 128, SPAN),
            vm(KEYS, 128, dtype=F32), vm(NS, 4, 128), vm(128, 128, dtype=F32), vm(128, 128),
            vm(128, 128, dtype=F32), vm(NR, 128, dtype=F32), vm(NR, 128, dtype=F32), vm(512, 128), vm(128, 512),
            vm(16, 128, 128), vm(16, 2, 128, dtype=F32), vm(16, 128, 128), vm(16, 2, 128, dtype=F32),
            vm(NX, NY, 128, 128), vm(NX, NY, 128, 128), vm(NY, 128, 128), vm(NY, 128, 128),
            vm(NS, 4, 128), vm(1, 128, dtype=F32), vm(NS, 1, 128, dtype=F32), vm(128, 128), vm(4, 128, 128),
            vm(16, 32, 512), vm(2, 16, 32, 512), vm(NX, 1024, 256), vm(NX, 128, 1024),
            vm(NX, 512, 256), vm(NX, 512, 256), vm(512, 128), vm(NX, 512, 128), vm(512, 512), vm(512, 512),
            vm(16, 32, 512), vm(16, 32, 512), vm(NS, 4, 512), vm(NS, 4, 512),
            dma(NY), dma(NY), dma(NY, NX), dma(NY, NX), dma(4), dma(4), dma(NS), dma(NS),
            dma(16), dma(16), dma(16), dma(16), dma(NX, NY), dma(NX, NY), dma(NY), dma(NY),
            dma(NS), dma(NS), dma(NS), dma(NS), dma(4), dma(4), dma(NR), dma(NR), dma(NR), dma(NR),
            dma(4), dma(4), dma(4), dma(4), dma(4), dma(4), dma(NX, CHUNKS), dma(NX, CHUNKS),
            dma(NX, CHUNKS), dma(NX, CHUNKS), dma(CHUNKS), dma(CHUNKS), dma(NR), dma(NR), dma(NS), dma(NS), dma(3),
        ],
        compiler_params=pltpu.CompilerParams(collective_id=0, has_side_effects=True),
    )(
        queries[0], kv_in, tree_in, resid[0], tree_parents, context_lengths,
        expert_ids[0].T, gate_weights[0].T, norm_gain.reshape(1, 4096), out_weight,
        w_gate[0].reshape(NX, 1024, 128), w_up[0].reshape(NX, 1024, 128), w_down[0],
    )
    return a_out[None], e_out[None]


def solution(mesh):
    placed = (
        P("req", "seq", None),
        P("req", "seq", None, None),
        P("req", "seq", None, None),
        P("req"),
        P("req", None),
        P("req", "seq", None),
        P("seq", None),
        P(),
        P("req", None, None),
        P("req", None, None),
        P(("req", "seq"), None, None),
        P(("req", "seq"), None, None),
        P(("req", "seq"), None, None),
    )
    return jax.shard_map(
        body,
        mesh=mesh,
        in_specs=placed,
        out_specs=(P("req", "seq", None), P("req", "seq", None)),
        check_vma=False,
    )
```

```python
import math

import jax
import jax.numpy as jnp
from jax import lax
from jax.experimental import pallas as pl
from jax.experimental.pallas import tpu as pltpu
from jax.sharding import PartitionSpec as P

BF = jnp.bfloat16
F32 = jnp.float32
MESH = pl.DeviceIdType.MESH
NX, NY = 4, 8
NR, NS = 16, 32
SPAN = 528
KEYS = 2 * SPAN
CHUNKS = 4
ASKS = NR // CHUNKS
SEATS = 32 * ASKS
STEPS = "FFFGFGGHGHDHDRHDRDRR"
CHUNK_OF = "01203120310210321323"
TEMPER = 128 ** (-0.5) * math.log2(math.e)
MASKED = -1e30
FLOOR = -1e29
EPS = 1e-06


def rem(a, b):
    return lax.rem(a, jnp.int32(b))


def div(a, b):
    return lax.div(a, jnp.int32(b))


def place():
    r = lax.axis_index("req")
    s = lax.axis_index("seq")
    return r, s, rem(s, NX), div(s, NX)


def remote(src, dst, send, recv, r, s):
    return pltpu.make_async_remote_copy(
        src_ref=src, dst_ref=dst, send_sem=send, recv_sem=recv, device_id=(r, s), device_id_type=MESH
    )


def loop(n, first=0):
    def run(fn):
        def step(i, c):
            fn(i)
            return c

        lax.fori_loop(first, n, step, 0)

    return run


def dot(a, b):
    return jnp.dot(a, b, preferred_element_type=F32)


def spread_of(o, n):
    o = n - 1 - o
    half = div(o + 1, 2)
    return jnp.where(rem(o, 2) == 1, half, rem(n - half, n))


def reach_of(o):
    return jnp.where(o < 4, spread_of(NR - 1 - o, NR), spread_of(o - 4, NR))


FAR = (4, 3, 5, 2, 6, 1, 7, 0)


def lanes(first, size):
    return pl.ds(pl.multiple_of(first, 128), size)


def part_of(g):
    return slice(128 * g, 128 * g + 128)


def seats_of(g):
    return slice(SEATS * g, SEATS * g + SEATS)


def asks_of(g):
    return range(max(ASKS * g, 1), ASKS * g + ASKS)


def layer_kernel(
    q, kv_in, tree_in, res, parents, length, ids, gates, gain, w_out, w_gate, w_up, w_down,
    a_out, e_out,
    qy, q_got, qf, kt, k, v, vt, bias, res_got, rf, reach, reach_f, chosen, rates, sel, back,
    out_src, st_src, got, got_st, p_src, p_got, y_src, y_got, a_src, sq_src, sq, mid_src, mid_q,
    d_src, rows, wgu, wd, gu_src, gu, hid_src, hid, pair_src, pair, ret_src, ret, f_src, fin,
    qys, qyr, qxs, qxr, ks, kr, rs, rr,
    hs, hr, ts, tr, ps, pr, ys, yr, as_, ar, qs, qr, ms, mr, zs, zr, fs, fr,
    gs, gr, us, ur, ds_, dr, gus, gur, hds, hdr, pas, par, bs, br, es, er, ls,
):
    r, s, x, y = place()
    b = rem(y, 2)
    h = b
    j = div(y, 2)
    top = div(y, 4)
    mate = s + NX - 2 * NX * b
    number = div(y, 2) * NX + x
    barrier = pltpu.get_barrier_semaphore()

    @loop(NS, 1)
    def _(d):
        pl.semaphore_signal(barrier, inc=1, device_id=(r, rem(s + d, NS)), device_id_type=MESH)

    @loop(NR, 1)
    def _(d):
        pl.semaphore_signal(barrier, inc=1, device_id=(rem(r + d, NR), s), device_id_type=MESH)

    def x_at(e):
        return rem(x + e, NX)

    def gate_copy(e, first=0, size=1024):
        to = x_at(e)
        span = pl.ds(first, size)
        return remote(w_gate.at[to, span], wgu.at[x, span, pl.ds(0, 128)], gs.at[e], gr.at[e], r, y * NX + to)

    def up_copy(e):
        to = x_at(e)
        return remote(w_up.at[to], wgu.at[x, :, pl.ds(128, 128)], us.at[e], ur.at[e], r, y * NX + to)

    def down_copy(e):
        to = x_at(e)
        return remote(w_down.at[:, lanes(to * 1024, 1024)], wd.at[x], ds_.at[e], dr.at[e], r, y * NX + to)

    own_g = pltpu.make_async_copy(w_gate.at[x], wgu.at[x, :, pl.ds(0, 128)], ls.at[0])
    own_u = pltpu.make_async_copy(w_up.at[x], wgu.at[x, :, pl.ds(128, 128)], ls.at[1])
    own_d = pltpu.make_async_copy(w_down.at[:, lanes(x * 1024, 1024)], wd.at[x], ls.at[2])
    own_g.start()
    own_u.start()
    own_d.start()

    mine_q = lanes(h * 2048, 2048)

    def qy_copy(d):
        to = rem(y + spread_of(d, NY), NY)
        return remote(q.at[:, lanes(rem(to, 2) * 2048, 2048)], qy.at[y], qys.at[d], qyr.at[d], r, to * NX + x)

    def qx_copy(d, e):
        row = rem(y + NY - spread_of(d, NY), NY)
        return remote(qy.at[row], q_got.at[row * NX + x], qxs.at[d, e], qxr.at[d, e], r, y * NX + x_at(e))

    def first_copy(e):
        return remote(q.at[:, mine_q], q_got.at[s], qxs.at[NY - 1, e], qxr.at[NY - 1, e], r, y * NX + x_at(e))

    def kv_copies():
        ctx, new = pl.ds(0, 512), pl.ds(512, 16)
        return (
            remote(kv_in.at[1 - h], kt.at[h], ks.at[0], kr.at[0], r, mate),
            remote(kv_in.at[3 - h], vt.at[h, :, ctx], ks.at[1], kr.at[1], r, mate),
            remote(tree_in.at[1 - h], k.at[h, new], ks.at[2], kr.at[2], r, mate),
            remote(tree_in.at[3 - h], v.at[h], ks.at[3], kr.at[3], r, mate),
        )

    def column(to):
        return lanes(rem(to, NX) * 1024 + div(to, NX) * 128, 128)

    def res_copy(d):
        to = rem(s + spread_of(d, NS), NS)
        return remote(res.at[:, column(to)], res_got.at[s], rs.at[d], rr.at[d], r, to)

    pl.semaphore_wait(barrier, NS + NR - 2)

    @loop(NY - 1)
    def _(d):
        qy_copy(d).start()

    for e in (2, 1, 3):
        first_copy(e).start()
    for copy in kv_copies():
        copy.start()
    q_got[s] = q[:, mine_q]
    kt[h] = kv_in[h]
    k[h, 512:528] = tree_in[h]
    vt[h, :, 0:512] = kv_in[2 + h]
    v[h] = tree_in[2 + h]
    res_got[s] = res[:, column(s)]

    for o in range(NR):
        hit = ids[...] == 4 * rem(r + reach_of(jnp.int32(o)), NR) + j
        chosen[o : o + 1, :] = jnp.sum(jnp.where(hit, 1.0, 0.0), axis=0, keepdims=True)
        rates[o : o + 1, :] = jnp.sum(jnp.where(hit, gates[...].astype(F32), 0.0), axis=0, keepdims=True)

    @loop(NY - 1)
    def _(d):
        qy_copy(d).wait_recv()
        for e in (2, 1, 3):
            qx_copy(d, e).start()
        row = rem(y + NY - spread_of(d, NY), NY)
        q_got[row * NX + x] = qy[row]

    @loop(NS - 1)
    def _(d):
        res_copy(d).start()

    node = lax.broadcasted_iota(jnp.int32, (128, 128), 0)
    spot = lax.broadcasted_iota(jnp.int32, (128, 128), 1)
    reach[...] = jnp.where((parents[...] == node) | (node == spot), 1.0, 0.0).astype(BF)

    @loop(5)
    def _(i):
        reach[...] = jnp.minimum(dot(reach[...], reach[...]), 1.0).astype(BF)

    reach_f[...] = jnp.where(reach[...].astype(F32) > 0.5, 0.0, MASKED)
    base = s - NX * h
    spot = lax.broadcasted_iota(jnp.int32, (SPAN, 128), 0)
    for p in range(2):
        first = (base + NX * p) * 512
        eight = reach_f[pl.ds(pl.multiple_of(8 * (div(base, 2) + 2 * p), 8), 8), :]
        seen = (spot < 512) & (spot + first < length[0])
        bias[p * SPAN : (p + 1) * SPAN, :] = jnp.where(seen, 0.0, MASKED)
        bias[p * SPAN + 512 : p * SPAN + 516, :] = jnp.where(rem(base, 2) == 1, eight[4:8, :], eight[0:4, :])

    earlier = lax.broadcasted_iota(jnp.int32, (128, 128), 0) < lax.broadcasted_iota(jnp.int32, (128, 128), 1)
    slot = dot(chosen[...].astype(BF), jnp.where(earlier, 1.0, 0.0).astype(BF))
    seat = lax.broadcasted_iota(jnp.int32, (32, 128), 0).astype(F32)
    for g in range(4):
        tall = []
        for o in range(4 * g, 4 * g + 4):
            hit = (slot[o : o + 1, :] == seat) & (chosen[o : o + 1, :] > 0.5)
            tall.append(jnp.where(hit, rates[o : o + 1, :], 0.0))
            sel[32 * o : 32 * o + 32, :] = jnp.where(hit, 1.0, 0.0).astype(BF)
        back[:, part_of(g)] = jnp.transpose(jnp.concatenate(tall, axis=0)).astype(BF)

    for copy in kv_copies():
        copy.wait()
    for p in range(2):
        for t in range(4):
            k[p, part_of(t), :] = jnp.transpose(kt[p, :, part_of(t)].astype(F32)).astype(BF)
        last = jnp.concatenate([v[p].astype(F32), jnp.zeros((112, 128), F32)], axis=0)
        vt[p, :, 512:528] = jnp.transpose(last)[:, 0:16].astype(BF)
    for e in range(1, NX):
        first_copy(e).wait()

    @loop(NY - 1)
    def _(d):
        qy_copy(d).wait_send()
        for e in range(1, NX):
            qx_copy(d, e).wait()

    for t in range(NS):
        qf[4 * t : 4 * t + 4, :] = q_got[t].astype(F32)

    def out_copy(i):
        return remote(out_src.at[i], got.at[number], hs.at[i], hr.at[number], r, 16 * h + i)

    def st_copy(i):
        return remote(st_src.at[i], got_st.at[number], ts.at[i], tr.at[number], r, 16 * h + i)

    def pair_at(n):
        return rem(n + div(number, 2), 8)

    def send_head(i):
        @pl.when(16 * h + i != s)
        def _():
            out_copy(i).start()
            st_copy(i).start()

        @pl.when(16 * h + i == s)
        def _():
            got[number] = out_src[i]
            got_st[number] = st_src[i]

    @loop(8)
    def _(n):
        p = pair_at(n)
        two = qf[:, lanes(p * 256, 256)].astype(BF)
        heads = jnp.concatenate([two[:, 0:128], two[:, 128:256]], axis=0)
        score = lax.dot_general(
            k[...].reshape(KEYS, 128), heads, (((1,), (1,)), ((), ())), preferred_element_type=F32
        )
        mask = bias[...]
        score = jnp.concatenate([score[:, 0:128] + mask, score[:, 128:256] + mask], axis=1)
        peak = jnp.maximum(jnp.max(score, axis=0, keepdims=True), FLOOR)
        prob = jnp.exp2((score - peak) * TEMPER)
        total = jnp.sum(prob, axis=0, keepdims=True)
        prob = prob.astype(BF)
        out = (dot(vt[0], prob[:SPAN]) + dot(vt[1], prob[SPAN:])).astype(BF)
        for t in range(2):
            out_src[2 * p + t] = out[:, part_of(t)]
            st_src[2 * p + t] = jnp.concatenate([peak[:, part_of(t)], total[:, part_of(t)]], axis=0)

        @pl.when(n >= 1)
        def _():
            send_head(2 * pair_at(n + 7))
            send_head(2 * pair_at(n + 7) + 1)

        for e in (1, 3):
            gate_copy(jnp.int32(e), pl.multiple_of(128 * n, 128), 128).start()

    send_head(2 * pair_at(jnp.int32(7)))
    send_head(2 * pair_at(jnp.int32(7)) + 1)
    gate_copy(jnp.int32(2)).start()

    @loop(NS - 1)
    def _(d):
        res_copy(d).wait()

    for t in range(NS):
        rf[4 * t : 4 * t + 4, :] = res_got[t].astype(F32)

    @loop(16)
    def _(n):
        who = (2 * div(n, NX) + top) * NX + rem(n, NX)

        @pl.when(who != s)
        def _():
            remote(out_src.at[0], got.at[n], hs.at[0], hr.at[n], r, who).wait_recv()
            remote(st_src.at[0], got_st.at[n], ts.at[0], tr.at[n], r, who).wait_recv()

    peaks = got_st[:, 0:1, :]
    totals = got_st[:, 1:2, :]
    peak = jnp.max(peaks, axis=0)
    factor = jnp.exp2((peaks - peak[None]) * TEMPER)
    denom = jnp.sum(factor * totals, axis=0)
    numer = jnp.zeros((128, 128), F32)
    for n in range(16):
        numer = numer + factor[n] * got[n].astype(F32)
    att = jnp.transpose(numer / denom).astype(BF)

    def p_copy(e, n):
        t = rem(y + FAR[n], NY)
        return remote(p_src.at[e, t], p_got.at[e, t], ps.at[e, n], pr.at[e, n], r, y * NX + x_at(e))

    for e in (2, 1, 3, 0):
        block = dot(att, w_out[:, lanes(x_at(jnp.int32(e)) * 1024, 1024)]).astype(BF)
        for t in range(NY):
            p_src[e, t] = block[:, part_of(t)]
    for n in range(NY):
        for e in (2, 1, 3):
            p_copy(e, n).start()
    up_copy(jnp.int32(2)).start()

    def y_copy(n):
        to = rem(y + FAR[n], NY)
        return remote(y_src.at[n], y_got.at[n], ys.at[n], yr.at[n], r, to * NX + x)

    for n in range(NY):
        t = rem(y + FAR[n], NY)
        acc = p_src[0, t].astype(F32)
        for e in range(1, NX):
            p_copy(e, n).wait_recv()
            acc = acc + p_got[e, t].astype(F32)
        if FAR[n]:
            y_src[n] = acc.astype(BF)
            y_copy(n).start()
    for n in range(NY - 1):
        y_copy(n).wait_recv()
        acc = acc + y_got[n].astype(F32)
    attended = acc.astype(BF)
    wide = attended.astype(F32)
    mid = (rf[...] + wide).astype(BF)
    midf = mid.astype(F32)
    mid_src[...] = mid
    col = jnp.sum(midf * midf, axis=1, keepdims=True)
    sq_src[...] = jnp.transpose(jnp.broadcast_to(col, (128, 128)))[0:1, :]
    sq[s] = sq_src[...]

    def mid_copy(n):
        to = (2 * n + top) * NX + x
        return remote(mid_src, mid_q.at[rem(y, 4)], ms.at[n], mr.at[rem(y, 4)], r, to)

    def sq_copy(d):
        return remote(sq_src, sq.at[s], qs.at[d], qr.at[d], r, rem(s + spread_of(d, NS), NS))

    def a_copy(d):
        to = rem(s + spread_of(d, NS), NS)
        return remote(a_src.at[to], a_out.at[:, column(s)], as_.at[d], ar.at[d], r, to)

    @loop(NS - 1)
    def _(d):
        sq_copy(d).start()

    @loop(4)
    def _(n):
        @pl.when(2 * n + top != y)
        def _():
            mid_copy(n).start()

        @pl.when(2 * n + top == y)
        def _():
            mid_q[rem(y, 4)] = mid_src[...]

    for t in range(NS):
        a_src[t] = wide[4 * t : 4 * t + 4, :].astype(BF)
    a_out[:, column(s)] = a_src[s]

    @loop(NS - 1)
    def _(d):
        a_copy(d).start()

    for e in (1, 3):
        up_copy(jnp.int32(e)).start()
    for e in (2, 1, 3):
        down_copy(jnp.int32(e)).start()

    @loop(4)
    def _(t):
        @pl.when(4 * b + t != y)
        def _():
            remote(mid_src, mid_q.at[t], ms.at[0], mr.at[t], r, (4 * b + t) * NX + x).wait_recv()

    @loop(NS - 1)
    def _(d):
        sq_copy(d).wait_recv()

    square = jnp.sum(sq[...], axis=0)
    scale = lax.rsqrt(square * (1.0 / 4096.0) + EPS)
    scale = jnp.transpose(jnp.broadcast_to(scale, (128, 128)))
    half = x * 2 + b

    def z_copy(o):
        to = rem(r + reach_of(o), NR)
        return remote(d_src.at[o], rows.at[b, o], zs.at[o], zr.at[o], to, s)

    def pass_copy(o):
        return remote(rows.at[b, o], rows.at[b, o], fs.at[o], fr.at[o], r, mate)

    def pass_got(o):
        return remote(rows.at[1 - b, o], rows.at[1 - b, o], fs.at[o], fr.at[o], r, mate)

    normed = jnp.concatenate(
        [
            (mid_q[t].astype(F32) * scale * gain[:, lanes(half * 512 + 128 * t, 128)].astype(F32)).astype(BF)
            for t in range(4)
        ], axis=1
    )
    for g in range(4):
        d_src[4 * g : 4 * g + 4] = dot(sel[part_of(g), :], normed).astype(BF).reshape(4, 32, 512)
        if g == 0:
            rows[b, 0] = d_src[0]
            pass_copy(jnp.int32(0)).start()
        for o in range(max(4 * g, 1), 4 * g + 4):
            z_copy(jnp.int32(o)).start()

    def gu_copy(e, g):
        return remote(
            gu_src.at[e, pl.ds(SEATS * g, SEATS)], gu.at[e, pl.ds(SEATS * g, SEATS)], gus.at[e, g], gur.at[e, g],
            r, y * NX + x_at(e),
        )

    def hid_copy(e, g):
        return remote(
            hid_src.at[pl.ds(SEATS * g, SEATS)], hid.at[x, pl.ds(SEATS * g, SEATS)], hds.at[e, g], hdr.at[e, g],
            r, y * NX + x_at(e),
        )

    def pair_copy(g):
        span = pl.ds(SEATS * g, SEATS)
        return remote(pair_src.at[span], pair.at[span], pas.at[g], par.at[g], r, mate)

    def b_copy(o):
        to = rem(r + NR - reach_of(o), NR)
        return remote(ret_src.at[o], ret.at[o], bs.at[o], br.at[o], to, s)

    def forward(g):
        for o in asks_of(g):
            z_copy(jnp.int32(o)).wait_recv()
            pass_copy(jnp.int32(o)).start()

    def gate_up(g):
        if g == 0:
            own_g.wait()
            own_u.wait()
            for e in range(1, NX):
                gate_copy(jnp.int32(e)).wait()
                up_copy(jnp.int32(e)).wait()
        for o in range(ASKS * g, ASKS * g + ASKS):
            pass_got(jnp.int32(o)).wait_recv()
        left = rows[0, ASKS * g : ASKS * g + ASKS].reshape(SEATS, 512)
        right = rows[1, ASKS * g : ASKS * g + ASKS].reshape(SEATS, 512)
        for e in (2, 1, 3, 0):
            to = x_at(jnp.int32(e))
            gu_src[e, seats_of(g), :] = (dot(left, wgu[to, 0:512, :]) + dot(right, wgu[to, 512:1024, :])).astype(BF)
            if e:
                gu_copy(e, g).start()

    def hidden(g):
        acc = gu_src[0, seats_of(g), :].astype(F32)
        for e in range(1, NX):
            gu_copy(e, g).wait_recv()
            acc = acc + gu[e, seats_of(g), :].astype(F32)
        gate = acc[:, 0:128]
        hid_src[seats_of(g), :] = (gate / (1.0 + jnp.exp(-gate)) * acc[:, 128:256]).astype(BF)
        for e in (2, 1, 3):
            hid_copy(e, g).start()
        hid[x, seats_of(g), :] = hid_src[seats_of(g), :]

    def product(g, side):
        cols = lanes(side * 512, 512)
        acc = dot(hid[0, seats_of(g), :], wd[0, :, cols])
        for t in range(1, NX):
            acc = acc + dot(hid[t, seats_of(g), :], wd[t, :, cols])
        return acc

    def down(g):
        if g == 0:
            own_d.wait()
            for e in range(1, NX):
                down_copy(jnp.int32(e)).wait()
        for e in range(1, NX):
            hid_copy(e, g).wait_recv()
        pair_src[seats_of(g), :] = product(g, 1 - b).astype(BF)
        pair_copy(g).start()

    def give(g):
        acc = product(g, b)
        pair_copy(g).wait_recv()
        acc = acc + pair[seats_of(g), :].astype(F32)
        ret_src[ASKS * g : ASKS * g + ASKS] = acc.astype(BF).reshape(ASKS, 32, 512)
        for o in asks_of(g):
            b_copy(jnp.int32(o)).start()
        if g == 0:
            ret[0] = ret_src[0]

    steps = {"F": forward, "G": gate_up, "H": hidden, "D": down, "R": give}
    for name, g in zip(STEPS, CHUNK_OF):
        steps[name](int(g))

    total = jnp.zeros((128, 512), F32)
    for g in range(4):
        for o in range(max(4 * g, 1), 4 * g + 4):
            b_copy(jnp.int32(o)).wait_recv()
        total = total + dot(back[:, part_of(g)], ret[4 * g : 4 * g + 4].reshape(128, 512))
    for t in range(NS):
        f_src[t] = total[4 * t : 4 * t + 4, :].astype(BF)

    def f_copy(d):
        to = rem(s + spread_of(d, NS), NS)
        return remote(f_src.at[to], fin.at[s], es.at[d], er.at[d], r, to)

    fin[s] = f_src[s]

    @loop(NS - 1)
    def _(d):
        f_copy(d).start()

    @loop(16)
    def _(i):
        @pl.when(16 * h + i != s)
        def _():
            out_copy(i).wait_send()
            st_copy(i).wait_send()

    for e in range(1, NX):
        for n in range(NY):
            p_copy(e, n).wait_send()
        for g in range(CHUNKS):
            gu_copy(e, g).wait_send()
            hid_copy(e, g).wait_send()

    for n in range(NY - 1):
        y_copy(n).wait_send()

    @loop(4)
    def _(n):
        @pl.when(2 * n + top != y)
        def _():
            mid_copy(n).wait_send()

    @loop(NS - 1)
    def _(d):
        sq_copy(d).wait_send()
        a_copy(d).wait()

    @loop(NR, 1)
    def _(o):
        z_copy(o).wait_send()
        b_copy(o).wait_send()

    @loop(NR)
    def _(o):
        pass_copy(o).wait_send()

    for g in range(CHUNKS):
        pair_copy(g).wait_send()

    @loop(NS - 1)
    def _(d):
        f_copy(d).wait()

    for xx in range(NX):
        for bb in range(2):
            acc = fin[bb * NX + xx].astype(F32)
            for n in range(1, 4):
                acc = acc + fin[(2 * n + bb) * NX + xx].astype(F32)
            e_out[:, 1024 * xx + 512 * bb : 1024 * xx + 512 * bb + 512] = acc.astype(BF)


VM = pl.BlockSpec(memory_space=pltpu.VMEM)
HB = pl.BlockSpec(memory_space=pl.ANY)


def sds(shape, dtype=BF):
    return jax.ShapeDtypeStruct(shape, dtype)


def dma(*shape):
    return pltpu.SemaphoreType.DMA(shape)


def vm(*shape, dtype=BF):
    return pltpu.VMEM(shape, dtype)


def body(
    queries, kv_cache, tree_kv, context_lengths, tree_parents, resid, out_weight, norm_gain,
    expert_ids, gate_weights, w_gate, w_up, w_down,
):
    kv_in = kv_cache[0].reshape(512, 4, 128).transpose(1, 2, 0)
    tree_in = jnp.pad(tree_kv[0].reshape(4, 4, 128).transpose(1, 0, 2), ((0, 0), (0, 12), (0, 0)))
    a_out, e_out = pl.pallas_call(
        layer_kernel,
        name="layer",
        out_shape=(sds((4, 4096)), sds((4, 4096))),
        in_specs=[VM] * 5 + [pl.BlockSpec(memory_space=pltpu.SMEM)] + [VM] * 4 + [HB] * 3,
        out_specs=(VM, VM),
        scratch_shapes=[
            vm(NY, 4, 2048), vm(NS, 4, 2048), vm(128, 2048, dtype=F32), vm(2, 128, 512), vm(2, SPAN, 128), vm(2, 16, 128), vm(2, 128, SPAN),
            vm(KEYS, 128, dtype=F32), vm(NS, 4, 128), vm(128, 128, dtype=F32), vm(128, 128),
            vm(128, 128, dtype=F32), vm(NR, 128, dtype=F32), vm(NR, 128, dtype=F32), vm(512, 128), vm(128, 512),
            vm(16, 128, 128), vm(16, 2, 128, dtype=F32), vm(16, 128, 128), vm(16, 2, 128, dtype=F32),
            vm(NX, NY, 128, 128), vm(NX, NY, 128, 128), vm(NY, 128, 128), vm(NY, 128, 128),
            vm(NS, 4, 128), vm(1, 128, dtype=F32), vm(NS, 1, 128, dtype=F32), vm(128, 128), vm(4, 128, 128),
            vm(16, 32, 512), vm(2, 16, 32, 512), vm(NX, 1024, 256), vm(NX, 128, 1024),
            vm(NX, 512, 256), vm(NX, 512, 256), vm(512, 128), vm(NX, 512, 128), vm(512, 512), vm(512, 512),
            vm(16, 32, 512), vm(16, 32, 512), vm(NS, 4, 512), vm(NS, 4, 512),
            dma(NY), dma(NY), dma(NY, NX), dma(NY, NX), dma(4), dma(4), dma(NS), dma(NS),
            dma(16), dma(16), dma(16), dma(16), dma(NX, NY), dma(NX, NY), dma(NY), dma(NY),
            dma(NS), dma(NS), dma(NS), dma(NS), dma(4), dma(4), dma(NR), dma(NR), dma(NR), dma(NR),
            dma(4), dma(4), dma(4), dma(4), dma(4), dma(4), dma(NX, CHUNKS), dma(NX, CHUNKS),
            dma(NX, CHUNKS), dma(NX, CHUNKS), dma(CHUNKS), dma(CHUNKS), dma(NR), dma(NR), dma(NS), dma(NS), dma(3),
        ],
        compiler_params=pltpu.CompilerParams(collective_id=0, has_side_effects=True),
    )(
        queries[0], kv_in, tree_in, resid[0], tree_parents, context_lengths,
        expert_ids[0].T, gate_weights[0].T, norm_gain.reshape(1, 4096), out_weight,
        w_gate[0].reshape(NX, 1024, 128), w_up[0].reshape(NX, 1024, 128), w_down[0],
    )
    return a_out[None], e_out[None]


def solution(mesh):
    placed = (
        P("req", "seq", None),
        P("req", "seq", None, None),
        P("req", "seq", None, None),
        P("req"),
        P("req", None),
        P("req", "seq", None),
        P("seq", None),
        P(),
        P("req", None, None),
        P("req", None, None),
        P(("req", "seq"), None, None),
        P(("req", "seq"), None, None),
        P(("req", "seq"), None, None),
    )
    return jax.shard_map(
        body,
        mesh=mesh,
        in_specs=placed,
        out_specs=(P("req", "seq", None), P("req", "seq", None)),
        check_vma=False,
    )
```
